128 devices in a mesh: ctx: 16 (over z, y_hi, core), head: 8 (over y_lo, x).
Axes of the slice: x: 4, y: 4 (y_hi: 2, y_lo: 2; y = y_hi * 2 + y_lo), z: 4, core: 2. Of those that a mesh axis runs over, the one named last changes fastest.
Arguments:
- query: bfloat16 [8192, 64, 128], P('ctx', 'head'), may hold values from -8 to 8
- keys: bfloat16 [8192, 8, 128], P('ctx', 'head'), may hold values from -8 to 8
- values: bfloat16 [8192, 8, 128], P('ctx', 'head'), may hold values from -6 to 6
- k_scale: bfloat16 [32, 8], P('ctx', 'head'), may hold values from 0.59765625 to 1.59375
- v_scale: bfloat16 [32, 8], P('ctx', 'head'), may hold values from 0.5 to 2
- block_place: int32 [32], P('ctx'), may hold values from 0 to 31, as said below
- out_weight: bfloat16 [8192, 8192], P('head'), may hold values from -1 to 1
Outputs:
- mixed: bfloat16 [8192, 8192], P(('ctx', 'head'))
The draws below stay inside these ranges and needn't reach their ends.
Inputs may be any that keep to these rules, and one draw needn't show every extreme that they name: `block_place`: A permutation of the block indices in which entries 2r and 2r + 1 sum to 31 and entry 2r is below 16.
All inputs are finite; a program needn't handle non-finite values.
Results may differ from the reference program's by a relative error of at most 0.015.
Values may be sent and summed in bfloat16 or wider, within the bound.
No kernel may reach another device: no remote copies, remote signals or barrier semaphores. Data moves between devices by JAX's collectives and lax.ppermute only.
A program may use at most 128 MiB of HBM per device.

```python
import math
import jax
import jax.numpy as jnp
from jax import lax

HQ = 64
KVH = 8
DH = 128
D = 8192
BLK = 256
NBLOCK = 32
TOKENS = 8192
HEAD_DEV = 8
N_HEAD = 8


def draw_query(key, part):
    shape = (TOKENS, HQ, DH)
    result = jnp.clip(jax.random.normal(jax.random.fold_in(key, 1), shape, jnp.float32), -6.0, 6.0)
    return result.astype(jnp.bfloat16)


def draw_keys(key, part):
    shape = (TOKENS, KVH, DH)
    result = jnp.clip(jax.random.normal(jax.random.fold_in(key, 2), shape, jnp.float32), -6.0, 6.0)
    return result.astype(jnp.bfloat16)


def draw_block_place(key, part):
    shuffled = jax.random.permutation(jax.random.fold_in(key, 3), NBLOCK // 2).astype(jnp.int32)
    return jnp.stack([shuffled, NBLOCK - 1 - shuffled], axis=1).reshape(NBLOCK).astype(jnp.int32)


def block_scale(rng, shape, pieces, smallest, high):
    level, own = 1.0, jax.random.fold_in(rng, 6)
    for dim, blocks in pieces:
        draws = jnp.exp(jax.random.uniform(jax.random.fold_in(own, dim), (blocks,), jnp.float32, smallest / len(pieces), high / len(pieces)))
        level = level * jnp.repeat(draws, shape[dim] // blocks).reshape([-1 if axis == dim else 1 for axis in range(len(shape))])
    return level


def normal_values(stream_key, extent, spread, most, cuts=(), held_as=jnp.bfloat16):
    values = jax.random.normal(stream_key, extent, jnp.float32) * spread
    if len(cuts) > 0:
        values = block_scale(stream_key, extent, cuts, -0.22, 0.18) * values
    return jnp.clip(values, min=-most, max=most).astype(held_as)


def setup_inputs(seed: int = 0) -> dict:
    splits = jax.random.split(jax.random.key(seed), 8)
    query = draw_query(jax.random.fold_in(splits[7], 71), 0)
    keys = draw_keys(jax.random.fold_in(splits[7], 71), 0)
    values = normal_values(splits[2], (TOKENS, KVH, DH), 1.0, 6.0, ((0, 16), (1, 8)))
    k_scale = jnp.clip(jnp.exp(math.log(1.59375) - 0.98082925 * jax.random.uniform(splits[3], (NBLOCK, KVH), jnp.float32) ** block_scale(splits[3], (NBLOCK, KVH), ((0, 16), (1, 8)), -0.2, 0.2)), 0.59765625, 1.59375).astype(jnp.bfloat16)
    v_scale = jnp.clip(jnp.exp(math.log(2.0) - 1.3862944 * jax.random.uniform(splits[4], (NBLOCK, KVH), jnp.float32) ** block_scale(splits[4], (NBLOCK, KVH), ((0, 16), (1, 8)), -0.2, 0.2)), 0.5, 2.0).astype(jnp.bfloat16)
    block_place = draw_block_place(jax.random.fold_in(splits[7], 71), 0)
    out_weight = normal_values(splits[6], (HQ * DH, D), (HQ * DH // 256) ** -0.5, 1.0, ((0, 8),))
    return {"query": query, "keys": keys, "values": values, "k_scale": k_scale, "v_scale": v_scale, "block_place": block_place, "out_weight": out_weight}


masked_value = -1e+30

def reference(query, keys, values, k_scale, v_scale, block_place, out_weight):
    group_size = HQ // KVH
    inv_root = 1.0 / math.sqrt(DH)
    token_place = (block_place[:, None] * BLK + jnp.arange(BLK, dtype=jnp.int32)[None, :]).reshape(TOKENS).astype(jnp.int32)
    key_gain = jnp.repeat(k_scale.astype(jnp.float32), BLK, axis=0)
    value_gain = jnp.repeat(v_scale.astype(jnp.float32), BLK, axis=0)

    def one_block(item_index):
        block_id = item_index // KVH
        group_id = item_index % KVH
        picked = lax.dynamic_slice(query, (block_id * BLK, group_id * group_size, jnp.int32(0)), (BLK, group_size, DH)).astype(jnp.float32)
        key_rows = lax.dynamic_slice_in_dim(keys, group_id, 1, 1)[:, 0, :].astype(jnp.float32)
        value_rows = lax.dynamic_slice_in_dim(values, group_id, 1, 1)[:, 0, :].astype(jnp.float32)
        key_column = lax.dynamic_slice_in_dim(key_gain, group_id, 1, 1)[:, 0]
        value_column = lax.dynamic_slice_in_dim(value_gain, group_id, 1, 1)[:, 0]
        scores = jnp.einsum('qrd,kd->rqk', picked, key_rows, precision=lax.Precision.HIGHEST)
        scores = scores * (key_column * inv_root)[None, None, :]
        query_place = lax.dynamic_slice_in_dim(token_place, block_id * BLK, BLK)
        visible = query_place[:, None] >= token_place[None, :]
        scores = jnp.where(visible[None], scores, masked_value)
        largest = lax.optimization_barrier(jnp.max(scores, axis=-1, keepdims=True))
        weights = jnp.exp(scores - largest)
        totals = lax.optimization_barrier(jnp.sum(weights, axis=-1))
        rounded = lax.optimization_barrier(weights.astype(jnp.bfloat16)).astype(jnp.float32)
        scaled_values = value_rows * value_column[:, None]
        summed = jnp.einsum('rqk,kd->rqd', rounded, scaled_values, precision=lax.Precision.HIGHEST)
        return (summed / totals[..., None]).astype(jnp.bfloat16)
    blocks = lax.map(one_block, jnp.arange(NBLOCK * KVH, dtype=jnp.int32))
    attended = blocks.reshape(NBLOCK, KVH, group_size, BLK, DH).transpose(0, 3, 1, 2, 4).reshape(TOKENS, HQ * DH)
    slab_width = HEAD_DEV * DH

    def add_group(running, group_index):
        part_rows = lax.dynamic_slice_in_dim(attended, group_index * slab_width, slab_width, 1)
        part_weight = lax.dynamic_slice_in_dim(out_weight, group_index * slab_width, slab_width, 0)
        group_term = jnp.dot(part_rows, part_weight, preferred_element_type=jnp.float32)
        rounded_term = lax.optimization_barrier(group_term.astype(jnp.bfloat16))
        return (running + rounded_term.astype(jnp.float32), None)
    summed_all, unused = lax.scan(add_group, jnp.zeros((TOKENS, D), jnp.float32), jnp.arange(N_HEAD, dtype=jnp.int32))
    return summed_all.astype(jnp.bfloat16)
```

```python
import itertools
import math

import jax
import jax.numpy as jnp
from jax import lax
from jax.experimental import pallas as pl
from jax.experimental.pallas import tpu as pltpu
from jax.sharding import PartitionSpec as P

F32 = jnp.float32
BF16 = jnp.bfloat16
AXES = ("ctx", "head")
NEG = -1e30
CHUNK = 128
NT = (((1,), (1,)), ((), ()))
NN = (((1,), (0,)), ((), ()))
META = 16


def index_of(z, yh, c, yl, x):
    return ((z % 4) * 4 + (yh % 2) * 2 + c % 2) * 8 + (yl % 2) * 4 + x % 4


def moved(array, step):
    pairs = []
    for z, yh, c, yl, x in itertools.product(range(4), range(2), range(2), range(2), range(4)):
        target = tuple(a + b for a, b in zip((z, yh, c, yl, x), step))
        pairs.append((index_of(z, yh, c, yl, x), index_of(*target)))
    return lax.ppermute(array, AXES, pairs)


def attend_rows(q_ref, acc_ref, l_ref, m_ref, base, count, keys, vals, gains, first=False, visible=None):
    width = keys.shape[0]
    for j in range(count):
        rows = pl.ds(pl.multiple_of(base + j * CHUNK, CHUNK), CHUNK)
        scores = lax.dot_general(q_ref[rows, :], keys, NT, preferred_element_type=F32) * gains
        if visible is not None:
            scores = jnp.where(visible(j), scores, NEG)
        top = jnp.max(scores, axis=1, keepdims=True)
        if first:
            new_m = jnp.broadcast_to(top, (CHUNK, 128))
        else:
            old_m = m_ref[rows, :]
            new_m = jnp.maximum(old_m, top)
        weights = jnp.exp2(scores - jnp.tile(new_m, (1, width // 128)))
        product = lax.dot_general(weights.astype(BF16), vals, NN, preferred_element_type=F32)
        if first:
            acc_ref[rows, :] = product[:, :128]
            l_ref[rows, :] = product[:, 128:]
        else:
            factor = jnp.exp2(old_m - new_m)
            acc_ref[rows, :] = acc_ref[rows, :] * factor + product[:, :128]
            l_ref[rows, :] = l_ref[rows, :] * factor + product[:, 128:]
        m_ref[rows, :] = new_m


def own_steps(q_ref, acc_ref, l_ref, m_ref, own_ref, inv):
    ones = jnp.ones((256, 128), BF16)
    low_k, high_k = own_ref[0:256, :], own_ref[256:512, :]
    low_v = jnp.concatenate([own_ref[512:768, :], ones], axis=1)
    high_v = jnp.concatenate([own_ref[768:1024, :], ones], axis=1)
    low_g = own_ref[1024:1025, :].astype(F32) * inv
    high_g = own_ref[1025:1026, :].astype(F32) * inv

    def low_visible(j):
        token = j * (CHUNK // 8) + lax.broadcasted_iota(jnp.int32, (CHUNK, 256), 0) // 8
        return lax.broadcasted_iota(jnp.int32, (CHUNK, 256), 1) <= token

    def high_visible(j):
        token = 256 + j * (CHUNK // 8) + lax.broadcasted_iota(jnp.int32, (CHUNK, 512), 0) // 8
        return lax.broadcasted_iota(jnp.int32, (CHUNK, 512), 1) <= token

    attend_rows(
        q_ref, acc_ref, l_ref, m_ref, 0, 16, low_k, low_v, jnp.tile(low_g, (1, 2)), True, low_visible
    )
    attend_rows(
        q_ref,
        acc_ref,
        l_ref,
        m_ref,
        2048,
        16,
        jnp.concatenate([low_k, high_k], axis=0),
        jnp.concatenate([low_v, high_v], axis=0),
        jnp.concatenate([low_g, low_g, high_g, high_g], axis=1),
        True,
        high_visible,
    )


def place_of(ref):
    return jnp.max(ref[1026:1027, :].astype(F32)).astype(jnp.int32)


def other_steps(q_ref, acc_ref, l_ref, m_ref, own_place, refs, kbuf, vbuf, gbuf, inv):
    count = len(refs)
    vbuf[:, 128:] = jnp.ones((2 * count * 256, 128), BF16)
    highs = jnp.int32(count)
    lows = jnp.int32(0)

    def put(slot, ref, half):
        at = pl.ds(pl.multiple_of(slot * 256, 256), 256)
        kbuf[at, :] = ref[pl.ds(pl.multiple_of(half * 256, 256), 256), :]
        vbuf[at, :128] = ref[pl.ds(pl.multiple_of(512 + half * 256, 256), 256), :]
        gain = jnp.where(half == 0, ref[1024:1025, :].astype(F32), ref[1025:1026, :].astype(F32))
        gbuf[pl.ds(slot, 1), :] = gain * inv

    for i, ref in enumerate(refs):
        put(i, ref, 0)
    for ref in refs:
        is_low = (place_of(ref) < own_place).astype(jnp.int32)
        slot = jnp.where(is_low == 1, 2 * count - 1 - lows, highs)
        put(slot, ref, 1 - is_low)
        lows = lows + is_low
        highs = highs + 1 - is_low

    def step(i, carry):
        first = 2 * i
        mixed = (first + 1) == highs
        base = jnp.where(first + 1 < highs, 2048, 0)
        at = pl.multiple_of(i * 512, 512)
        g0 = gbuf[pl.ds(first, 1), :]
        g1 = gbuf[pl.ds(first + 1, 1), :]

        @pl.when(jnp.logical_not(mixed))
        def _():
            attend_rows(
                q_ref,
                acc_ref,
                l_ref,
                m_ref,
                base,
                16,
                kbuf[pl.ds(at, 512), :],
                vbuf[pl.ds(at, 512), :],
                jnp.concatenate([g0, g0, g1, g1], axis=1),
            )

        @pl.when(mixed)
        def _():
            attend_rows(
                q_ref,
                acc_ref,
                l_ref,
                m_ref,
                2048,
                16,
                kbuf[pl.ds(at, 256), :],
                vbuf[pl.ds(at, 256), :],
                jnp.concatenate([g0, g0], axis=1),
            )
            attend_rows(
                q_ref,
                acc_ref,
                l_ref,
                m_ref,
                0,
                16,
                kbuf[pl.ds(at + 256, 256), :],
                vbuf[pl.ds(at + 256, 256), :],
                jnp.concatenate([g1, g1], axis=1),
            )

        return carry

    lax.fori_loop(0, count, step, 0)


def group_kernel(inv, count, start, finish, *refs):
    refs = list(refs)
    q_ref = refs.pop(0)
    own_ref = refs.pop(0)
    others = [refs.pop(0) for _ in range(count)]
    if not start:
        del refs[:3]
    att_ref = refs.pop(0) if finish else None
    acc_ref, l_ref, m_ref, kbuf, vbuf, gbuf = refs
    if start:
        own_steps(q_ref, acc_ref, l_ref, m_ref, own_ref, inv)
    other_steps(q_ref, acc_ref, l_ref, m_ref, place_of(own_ref), others, kbuf, vbuf, gbuf, inv)
    if finish:
        acc_ref[...] = acc_ref[...] / l_ref[...]
        for h in range(8):
            rows = pl.ds(h, 512, stride=8)
            att_ref[:, h * 128 : (h + 1) * 128] = acc_ref[rows, :].astype(BF16)


def attend(q, own, others, state, finish, inv, name):
    count = len(others)
    start = state is None
    vmem = pl.BlockSpec(memory_space=pltpu.VMEM)
    shapes = [jax.ShapeDtypeStruct((4096, 128), F32)] * 3
    operands = [q, own, *others] + ([] if start else list(state))
    scratch = [
        pltpu.VMEM((2 * count * 256, 128), BF16),
        pltpu.VMEM((2 * count * 256, 256), BF16),
        pltpu.VMEM((2 * count, 128), F32),
    ]
    aliases = {}
    if finish:
        outs = [jax.ShapeDtypeStruct((512, 1024), BF16)]
        scratch = [pltpu.VMEM(s.shape, s.dtype) for s in shapes] + scratch
        if not start:
            outs = outs + shapes
            scratch = scratch[3:]
            aliases = {2 + count + i: 1 + i for i in range(3)}
    else:
        outs = shapes
        if not start:
            aliases = {2 + count + i: i for i in range(3)}
    tiles = 2 * count + (3 if start else 0)
    import functools

    return pl.pallas_call(
        functools.partial(group_kernel, inv, count, start, finish),
        out_shape=outs,
        in_specs=[vmem] * len(operands),
        out_specs=[vmem] * len(outs),
        scratch_shapes=scratch,
        input_output_aliases=aliases,
        compiler_params=pltpu.CompilerParams(vmem_limit_bytes=40 << 20),
        cost_estimate=pl.CostEstimate(
            flops=tiles * 4 * 2048 * 256 * 128 * 4,
            transcendentals=tiles * 2048 * 256,
            bytes_accessed=1 << 20,
        ),
        name=name,
    )(*operands)


def body(query, keys, values, k_scale, v_scale, block_place, out_weight):
    inv = math.log2(math.e) / math.sqrt(128)
    q = query.reshape(4096, 128)
    k = keys.reshape(512, 128)
    gain = jnp.repeat(v_scale.reshape(2).astype(F32), 256)[:, None]
    v = (values.reshape(512, 128).astype(F32) * gain).astype(BF16)
    meta = jnp.concatenate(
        [k_scale.reshape(2), block_place.astype(BF16), jnp.zeros((META - 4,), BF16)]
    )
    own = jnp.concatenate([k, v, jnp.broadcast_to(meta[:, None], (META, 128))], axis=0)
    swap = (0, 0, 1, 0, 0)
    partner = moved(own, swap)
    up = moved(own, (1, 0, 0, 0, 0))
    down = moved(own, (-1, 0, 0, 0, 0))
    over = moved(own, (0, 1, 0, 0, 0))
    far = moved(own, (2, 0, 0, 0, 0))
    up2, down2 = moved(up, swap), moved(down, swap)
    state = attend(q, own, [partner], None, False, inv, "attend_own")
    state = attend(q, own, [up, down, up2, down2], state, False, inv, "attend_near")
    over2, far2 = moved(over, swap), moved(far, swap)
    oup = moved(over, (1, 0, 0, 0, 0))
    odown = moved(over, (-1, 0, 0, 0, 0))
    ofar = moved(over, (2, 0, 0, 0, 0))
    state = attend(q, own, [over, far, over2, far2], state, False, inv, "attend_over")
    rest = [oup, odown, ofar]
    rest = rest + [moved(r, swap) for r in rest]
    attended = attend(q, own, rest, state, True, inv, "attend_rest")[0]
    return lax.psum_scatter(
        jnp.dot(attended, out_weight, preferred_element_type=F32).astype(BF16),
        "head",
        scatter_dimension=0,
        tiled=True,
    )


def solution(mesh):
    placed = (
        P("ctx", "head", None),
        P("ctx", "head", None),
        P("ctx", "head", None),
        P("ctx", "head"),
        P("ctx", "head"),
        P("ctx"),
        P("head", None),
    )
    return jax.shard_map(
        body, mesh=mesh, in_specs=placed, out_specs=P(("ctx", "head"), None), check_vma=False
    )
```

```python
import functools
import itertools
import math

import jax
import jax.numpy as jnp
from jax import lax
from jax.experimental import pallas as pl
from jax.experimental.pallas import tpu as pltpu
from jax.sharding import PartitionSpec as P

F32 = jnp.float32
BF16 = jnp.bfloat16
AXES = ("ctx", "head")
NEG = -1e30
CHUNK = 128
NT = (((1,), (1,)), ((), ()))
NN = (((1,), (0,)), ((), ()))
META = 16
PAYLOAD = 1024 + META


def index_of(z, yh, c, yl, x):
    return ((z % 4) * 4 + (yh % 2) * 2 + c % 2) * 8 + (yl % 2) * 4 + x % 4


def moved(array, target):
    pairs = []
    for at in itertools.product(range(4), range(2), range(2), range(2), range(4)):
        pairs.append((index_of(*at), index_of(*target(*at))))
    return lax.ppermute(array, AXES, pairs)


def swapped(z, yh, c, yl, x):
    return z, yh, 1 - c, yl, x


def near(z, yh, c, yl, x):
    return z + (1 if c == 0 else -1), yh, c, yl, x


def across(z, yh, c, yl, x):
    return (z, yh + 1, c, yl, x) if c == 0 else (z + 2, yh, c, yl, x)


def diagonal(z, yh, c, yl, x):
    return z + (1 if c == 0 else -1), yh + 1, c, yl, x


def opposite(z, yh, c, yl, x):
    return z + 2, yh + 1, c, yl, x


def ahead(z, yh, c, yl, x):
    return z, yh, c, yl, x + (1 if c == 0 else -1)


def behind(z, yh, c, yl, x):
    return z, yh, c, yl, x - (1 if c == 0 else -1)


def beside(z, yh, c, yl, x):
    return z, yh, c, yl + 1, x


def attend_rows(q_ref, acc_ref, l_ref, m_ref, base, count, keys, vals, gains, first=False, visible=None):
    width = keys.shape[0]
    for j in range(count):
        rows = pl.ds(pl.multiple_of(base + j * CHUNK, CHUNK), CHUNK)
        scores = lax.dot_general(q_ref[rows, :], keys, NT, preferred_element_type=F32) * gains
        if visible is not None:
            scores = jnp.where(visible(j), scores, NEG)
        top = jnp.max(scores, axis=1, keepdims=True)
        if first:
            new_m = jnp.broadcast_to(top, (CHUNK, 128))
        else:
            old_m = m_ref[rows, :]
            new_m = jnp.maximum(old_m, top)
        weights = jnp.exp2(scores - jnp.tile(new_m, (1, width // 128)))
        product = lax.dot_general(weights.astype(BF16), vals, NN, preferred_element_type=F32)
        if first:
            acc_ref[rows, :] = product[:, :128]
            l_ref[rows, :] = product[:, 128:]
        else:
            factor = jnp.exp2(old_m - new_m)
            acc_ref[rows, :] = acc_ref[rows, :] * factor + product[:, :128]
            l_ref[rows, :] = l_ref[rows, :] * factor + product[:, 128:]
        m_ref[rows, :] = new_m


def own_steps(q_ref, acc_ref, l_ref, m_ref, own_ref, inv):
    ones = jnp.ones((256, 128), BF16)
    low_k, high_k = own_ref[0:256, :], own_ref[256:512, :]
    low_v = jnp.concatenate([own_ref[512:768, :], ones], axis=1)
    high_v = jnp.concatenate([own_ref[768:1024, :], ones], axis=1)
    low_g = own_ref[1024:1025, :].astype(F32) * inv
    high_g = own_ref[1025:1026, :].astype(F32) * inv

    def low_visible(j):
        token = j * (CHUNK // 8) + lax.broadcasted_iota(jnp.int32, (CHUNK, 256), 0) // 8
        return lax.broadcasted_iota(jnp.int32, (CHUNK, 256), 1) <= token

    def high_visible(j):
        token = 256 + j * (CHUNK // 8) + lax.broadcasted_iota(jnp.int32, (CHUNK, 512), 0) // 8
        return lax.broadcasted_iota(jnp.int32, (CHUNK, 512), 1) <= token

    attend_rows(
        q_ref, acc_ref, l_ref, m_ref, 0, 16, low_k, low_v, jnp.tile(low_g, (1, 2)), True, low_visible
    )
    attend_rows(
        q_ref,
        acc_ref,
        l_ref,
        m_ref,
        2048,
        16,
        jnp.concatenate([low_k, high_k], axis=0),
        jnp.concatenate([low_v, high_v], axis=0),
        jnp.concatenate([low_g, low_g, high_g, high_g], axis=1),
        True,
        high_visible,
    )


def place_of(ref, offset=0):
    return jnp.max(ref[offset + 1026 : offset + 1027, :].astype(F32)).astype(jnp.int32)


def other_steps(q_ref, acc_ref, l_ref, m_ref, own_place, refs, kbuf, vbuf, gbuf, inv):
    count = len(refs)
    vbuf[:, 128:] = jnp.ones((2 * count * 256, 128), BF16)
    highs = jnp.int32(count)
    lows = jnp.int32(0)

    def put(slot, ref, offset, half):
        at = pl.ds(pl.multiple_of(slot * 256, 256), 256)
        source = pl.multiple_of(half * 256, 256)
        kbuf[at, :] = ref[pl.ds(offset + source, 256), :]
        vbuf[at, :128] = ref[pl.ds(offset + 512 + source, 256), :]
        gains = ref[offset + 1024 : offset + 1026, :].astype(F32)
        gbuf[pl.ds(slot, 1), :] = jnp.where(half == 0, gains[0:1], gains[1:2]) * inv

    for i, (ref, offset) in enumerate(refs):
        put(i, ref, offset, 0)
    for ref, offset in refs:
        is_low = (place_of(ref, offset) < own_place).astype(jnp.int32)
        slot = jnp.where(is_low == 1, 2 * count - 1 - lows, highs)
        put(slot, ref, offset, 1 - is_low)
        lows = lows + is_low
        highs = highs + 1 - is_low

    def step(i, carry):
        first = 2 * i
        mixed = (first + 1) == highs
        base = jnp.where(first + 1 < highs, 2048, 0)
        at = pl.multiple_of(i * 512, 512)
        g0 = gbuf[pl.ds(first, 1), :]
        g1 = gbuf[pl.ds(first + 1, 1), :]

        @pl.when(jnp.logical_not(mixed))
        def _():
            attend_rows(
                q_ref,
                acc_ref,
                l_ref,
                m_ref,
                base,
                16,
                kbuf[pl.ds(at, 512), :],
                vbuf[pl.ds(at, 512), :],
                jnp.concatenate([g0, g0, g1, g1], axis=1),
            )

        @pl.when(mixed)
        def _():
            attend_rows(
                q_ref,
                acc_ref,
                l_ref,
                m_ref,
                2048,
                16,
                kbuf[pl.ds(at, 256), :],
                vbuf[pl.ds(at, 256), :],
                jnp.concatenate([g0, g0], axis=1),
            )
            attend_rows(
                q_ref,
                acc_ref,
                l_ref,
                m_ref,
                0,
                16,
                kbuf[pl.ds(at + 256, 256), :],
                vbuf[pl.ds(at + 256, 256), :],
                jnp.concatenate([g1, g1], axis=1),
            )

        return carry

    lax.fori_loop(0, count, step, 0)


def group_kernel(inv, sizes, start, finish, *refs):
    refs = list(refs)
    q_ref = refs.pop(0)
    own_ref = refs.pop(0)
    order_ref = refs.pop(0) if finish else None
    others = []
    for size in sizes:
        ref = refs.pop(0)
        others += [(ref, i * PAYLOAD) for i in range(size)]
    if not start:
        del refs[:3]
    att_ref = refs.pop(0) if finish else None
    acc_ref, l_ref, m_ref, kbuf, vbuf, gbuf = refs
    if start:
        own_steps(q_ref, acc_ref, l_ref, m_ref, own_ref, inv)
    own_place = place_of(own_ref)
    other_steps(q_ref, acc_ref, l_ref, m_ref, own_place, others, kbuf, vbuf, gbuf, inv)
    if finish:
        acc_ref[...] = acc_ref[...] / l_ref[...]
        for block in range(8):
            target = pl.ds(pl.multiple_of(order_ref[block] * 64, 64), 64)
            for h in range(8):
                rows = pl.ds(block * 512 + h, 64, stride=8)
                att_ref[target, h * 128 : (h + 1) * 128] = acc_ref[rows, :].astype(BF16)


def attend(q, own, others, state, order, inv, name):
    sizes = [o.shape[0] // PAYLOAD for o in others]
    count = sum(sizes)
    start = state is None
    finish = order is not None
    vmem = pl.BlockSpec(memory_space=pltpu.VMEM)
    shapes = [jax.ShapeDtypeStruct((4096, 128), F32)] * 3
    operands = [q, own] + ([order] if finish else []) + list(others)
    specs = [vmem] * len(operands)
    if finish:
        specs[2] = pl.BlockSpec(memory_space=pltpu.SMEM)
    outs = ([jax.ShapeDtypeStruct((512, 1024), BF16)] if finish else []) + shapes
    aliases = {}
    if not start:
        shift = len(outs) - 3
        aliases = {len(operands) + i: shift + i for i in range(3)}
        operands += list(state)
        specs += [vmem] * 3
    tiles = 2 * count + (3 if start else 0)
    return pl.pallas_call(
        functools.partial(group_kernel, inv, sizes, start, finish),
        out_shape=outs,
        in_specs=specs,
        out_specs=[vmem] * len(outs),
        scratch_shapes=[
            pltpu.VMEM((2 * count * 256, 128), BF16),
            pltpu.VMEM((2 * count * 256, 256), BF16),
            pltpu.VMEM((2 * count, 128), F32),
        ],
        input_output_aliases=aliases,
        compiler_params=pltpu.CompilerParams(vmem_limit_bytes=32 << 20),
        cost_estimate=pl.CostEstimate(
            flops=tiles * 2048 * 256 * 128 * 16,
            transcendentals=tiles * 2048 * 256,
            bytes_accessed=1 << 20,
        ),
        name=name,
    )(*operands)


def project_kernel(blocks, splits, a_ref, w_ref, *o_refs):
    rows = jnp.concatenate([a_ref[b * 64 : (b + 1) * 64, :] for b in blocks], axis=0)
    product = jnp.dot(rows, w_ref[...], preferred_element_type=F32).astype(BF16)
    at = 0
    for size, o_ref in zip(splits, o_refs):
        o_ref[...] = product[at * 64 : (at + size) * 64, :]
        at += size


def project(att, weight, blocks, splits, first, columns, name):
    tile = 1024
    start = first // tile
    return pl.pallas_call(
        functools.partial(project_kernel, blocks, splits),
        out_shape=[jax.ShapeDtypeStruct((s * 64, columns), BF16) for s in splits],
        grid=(columns // tile,),
        in_specs=[
            pl.BlockSpec((512, 1024), lambda j: (0, 0)),
            pl.BlockSpec((1024, tile), lambda j: (0, j + start)),
        ],
        out_specs=[pl.BlockSpec((s * 64, tile), lambda j: (0, j)) for s in splits],
        compiler_params=pltpu.CompilerParams(vmem_limit_bytes=24 << 20),
        cost_estimate=pl.CostEstimate(
            flops=2 * len(blocks) * 64 * 1024 * columns,
            transcendentals=0,
            bytes_accessed=2 * 1024 * columns,
        ),
        name=name,
    )(att, weight)


def added(*arrays):
    total = arrays[0].astype(F32)
    for a in arrays[1:]:
        total = total + a.astype(F32)
    return total


def scattered(att, weight, first_columns):
    rest = weight.shape[1] - first_columns
    x_far, x_behind = project(att, weight, (0, 1, 4, 5), (2, 2), 0, first_columns, "project_a")
    got_far = moved(x_far, ahead)
    got_front = moved(x_behind, behind)
    (y_out,) = project(att, weight, (1, 3, 5, 7), (4,), first_columns, rest, "project_b")
    got_y = moved(y_out, beside)
    x_ahead, x_own = project(att, weight, (2, 3, 6, 7), (2, 2), 0, first_columns, "project_c")
    (y_own,) = project(att, weight, (0, 2, 4, 6), (4,), first_columns, rest, "project_d")
    got_back = moved(added(x_ahead, got_far).astype(BF16), ahead)
    y_far, y_ahead, y_behind, y_mine = [
        (y_own[i * 64 : (i + 1) * 64], got_y[i * 64 : (i + 1) * 64]) for i in range(4)
    ]
    y_got_far = moved(added(*y_far).astype(BF16), ahead)
    y_got_front = moved(added(*y_behind).astype(BF16), behind)
    y_got_back = moved(added(*y_ahead, y_got_far).astype(BF16), ahead)
    x_out = added(x_own[64:], got_front[64:], got_back[64:]).astype(BF16)
    x_last = moved(x_out, beside)
    return jnp.concatenate(
        [
            added(x_own[:64], got_front[:64], got_back[:64], x_last).astype(BF16),
            added(*y_mine, y_got_front, y_got_back).astype(BF16),
        ],
        axis=1,
    )


def body(query, keys, values, k_scale, v_scale, block_place, out_weight):
    inv = math.log2(math.e) / math.sqrt(128)
    q = query.reshape(4096, 128)
    k = keys.reshape(512, 128)
    gain = jnp.repeat(v_scale.reshape(2).astype(F32), 256)[:, None]
    v = (values.reshape(512, 128).astype(F32) * gain).astype(BF16)
    meta = jnp.concatenate(
        [k_scale.reshape(2), block_place.astype(BF16), jnp.zeros((META - 4,), BF16)]
    )
    own = jnp.concatenate([k, v, jnp.broadcast_to(meta[:, None], (META, 128))], axis=0)
    partner = moved(own, swapped)
    pair = jnp.concatenate([own, partner], axis=0)
    one, two, three = moved(pair, near), moved(pair, across), moved(pair, diagonal)
    four = moved(own, opposite)
    state = attend(q, own, [partner], None, None, inv, "attend_own")
    one, two, *state = lax.optimization_barrier((one, two, *state))
    more = moved(jnp.concatenate([one, two], axis=0), swapped)
    state = attend(q, own, [one, two], state, None, inv, "attend_near")
    three, four, *state = lax.optimization_barrier((three, four, *state))
    last = jnp.concatenate([three, four], axis=0)
    final = moved(last, swapped)
    state = attend(q, own, [more], state, None, inv, "attend_more")
    core = lax.axis_index("ctx") % 2
    place = lax.axis_index("head")
    target = jnp.arange(8, dtype=jnp.int32)
    along = (target % 4 - place % 4) % 4
    side = (target // 4 - place // 4) % 2
    forward = 1 + 2 * core
    slot = jnp.where(along == 0, 3, jnp.where(along == 2, 0, jnp.where(along == forward, 1, 2)))
    order = (slot * 2 + side).astype(jnp.int32)
    attended = attend(q, own, [last, final], state, order, inv, "attend_rest")[0]
    return scattered(attended, out_weight, 5120)


def solution(mesh):
    placed = (
        P("ctx", "head", None),
        P("ctx", "head", None),
        P("ctx", "head", None),
        P("ctx", "head"),
        P("ctx", "head"),
        P("ctx"),
        P("head", None),
    )
    return jax.shard_map(
        body, mesh=mesh, in_specs=placed, out_specs=P(("ctx", "head"), None), check_vma=False
    )
```

```python
import functools
import itertools
import math

import jax
import jax.numpy as jnp
from jax import lax
from jax.experimental import pallas as pl
from jax.experimental.pallas import tpu as pltpu
from jax.sharding import PartitionSpec as P

F32 = jnp.float32
BF16 = jnp.bfloat16
AXES = ("ctx", "head")
NEG = -1e30
CHUNK = 128
NT = (((1,), (1,)), ((), ()))
NN = (((1,), (0,)), ((), ()))
META = 16
PAYLOAD = 1024 + META
TILE = 512
LIMIT = 20 << 20


def index_of(z, yh, c, yl, x):
    return ((z % 4) * 4 + (yh % 2) * 2 + c % 2) * 8 + (yl % 2) * 4 + x % 4


def moved(array, target):
    pairs = []
    for at in itertools.product(range(4), range(2), range(2), range(2), range(4)):
        pairs.append((index_of(*at), index_of(*target(*at))))
    return lax.ppermute(array, AXES, pairs)


def swapped(z, yh, c, yl, x):
    return z, yh, 1 - c, yl, x


def near(z, yh, c, yl, x):
    return z + (1 if c == 0 else -1), yh, c, yl, x


def across(z, yh, c, yl, x):
    return (z, yh + 1, c, yl, x) if c == 0 else (z + 2, yh, c, yl, x)


def diagonal(z, yh, c, yl, x):
    return z + (1 if c == 0 else -1), yh + 1, c, yl, x


def opposite(z, yh, c, yl, x):
    return z + 2, yh + 1, c, yl, x


def ahead(z, yh, c, yl, x):
    return z, yh, c, yl, x + (1 if c == 0 else -1)


def behind(z, yh, c, yl, x):
    return z, yh, c, yl, x - (1 if c == 0 else -1)


def beside(z, yh, c, yl, x):
    return z, yh, c, yl + 1, x


def attend_rows(q_ref, acc_ref, l_ref, m_ref, base, count, keys, vals, gains, first=False, visible=None):
    width = keys.shape[0]
    for j in range(count):
        rows = pl.ds(pl.multiple_of(base + j * CHUNK, CHUNK), CHUNK)
        scores = lax.dot_general(q_ref[rows, :], keys, NT, preferred_element_type=F32) * gains
        if visible is not None:
            scores = jnp.where(visible(j), scores, NEG)
        top = jnp.max(scores, axis=1, keepdims=True)
        if first:
            new_m = jnp.broadcast_to(top, (CHUNK, 128))
        else:
            old_m = m_ref[rows, :]
            new_m = jnp.maximum(old_m, top)
        weights = jnp.exp2(scores - jnp.tile(new_m, (1, width // 128)))
        product = lax.dot_general(weights.astype(BF16), vals, NN, preferred_element_type=F32)
        if first:
            acc_ref[rows, :] = product[:, :128]
            l_ref[rows, :] = product[:, 128:]
        else:
            factor = jnp.exp2(old_m - new_m)
            acc_ref[rows, :] = acc_ref[rows, :] * factor + product[:, :128]
            l_ref[rows, :] = l_ref[rows, :] * factor + product[:, 128:]
        m_ref[rows, :] = new_m


def own_steps(q_ref, acc_ref, l_ref, m_ref, own_ref, inv):
    ones = jnp.ones((256, 128), BF16)
    low_k, high_k = own_ref[0:256, :], own_ref[256:512, :]
    low_v = jnp.concatenate([own_ref[512:768, :], ones], axis=1)
    high_v = jnp.concatenate([own_ref[768:1024, :], ones], axis=1)
    low_g = own_ref[1024:1025, :].astype(F32) * inv
    high_g = own_ref[1025:1026, :].astype(F32) * inv

    def low_visible(j):
        token = j * (CHUNK // 8) + lax.broadcasted_iota(jnp.int32, (CHUNK, 256), 0) // 8
        return lax.broadcasted_iota(jnp.int32, (CHUNK, 256), 1) <= token

    def high_visible(j):
        token = 256 + j * (CHUNK // 8) + lax.broadcasted_iota(jnp.int32, (CHUNK, 512), 0) // 8
        return lax.broadcasted_iota(jnp.int32, (CHUNK, 512), 1) <= token

    attend_rows(
        q_ref, acc_ref, l_ref, m_ref, 0, 16, low_k, low_v, jnp.tile(low_g, (1, 2)), True, low_visible
    )
    attend_rows(
        q_ref,
        acc_ref,
        l_ref,
        m_ref,
        2048,
        16,
        jnp.concatenate([low_k, high_k], axis=0),
        jnp.concatenate([low_v, high_v], axis=0),
        jnp.concatenate([low_g, low_g, high_g, high_g], axis=1),
        True,
        high_visible,
    )


def place_of(ref, offset=0):
    return jnp.max(ref[offset + 1026 : offset + 1027, :].astype(F32)).astype(jnp.int32)


def other_steps(q_ref, acc_ref, l_ref, m_ref, own_place, refs, kbuf, vbuf, gbuf, inv):
    count = len(refs)
    vbuf[:, 128:] = jnp.ones((2 * count * 256, 128), BF16)
    highs = jnp.int32(count)
    lows = jnp.int32(0)

    def put(slot, ref, offset, half):
        at = pl.ds(pl.multiple_of(slot * 256, 256), 256)
        source = pl.multiple_of(half * 256, 256)
        kbuf[at, :] = ref[pl.ds(offset + source, 256), :]
        vbuf[at, :128] = ref[pl.ds(offset + 512 + source, 256), :]
        gains = ref[offset + 1024 : offset + 1026, :].astype(F32)
        gbuf[pl.ds(slot, 1), :] = jnp.where(half == 0, gains[0:1], gains[1:2]) * inv

    for i, (ref, offset) in enumerate(refs):
        put(i, ref, offset, 0)
    for ref, offset in refs:
        is_low = (place_of(ref, offset) < own_place).astype(jnp.int32)
        slot = jnp.where(is_low == 1, 2 * count - 1 - lows, highs)
        put(slot, ref, offset, 1 - is_low)
        lows = lows + is_low
        highs = highs + 1 - is_low

    def step(i, carry):
        first = 2 * i
        mixed = (first + 1) == highs
        base = jnp.where(first + 1 < highs, 2048, 0)
        at = pl.multiple_of(i * 512, 512)
        g0 = gbuf[pl.ds(first, 1), :]
        g1 = gbuf[pl.ds(first + 1, 1), :]

        @pl.when(jnp.logical_not(mixed))
        def _():
            attend_rows(
                q_ref,
                acc_ref,
                l_ref,
                m_ref,
                base,
                16,
                kbuf[pl.ds(at, 512), :],
                vbuf[pl.ds(at, 512), :],
                jnp.concatenate([g0, g0, g1, g1], axis=1),
            )

        @pl.when(mixed)
        def _():
            attend_rows(
                q_ref,
                acc_ref,
                l_ref,
                m_ref,
                2048,
                16,
                kbuf[pl.ds(at, 256), :],
                vbuf[pl.ds(at, 256), :],
                jnp.concatenate([g0, g0], axis=1),
            )
            attend_rows(
                q_ref,
                acc_ref,
                l_ref,
                m_ref,
                0,
                16,
                kbuf[pl.ds(at + 256, 256), :],
                vbuf[pl.ds(at + 256, 256), :],
                jnp.concatenate([g1, g1], axis=1),
            )

        return carry

    lax.fori_loop(0, count, step, 0)


def pack_kernel(k_ref, v_ref, ks_ref, vs_ref, place_ref, o_ref):
    o_ref[0:512, :] = k_ref[...]
    for half in range(2):
        rows = slice(half * 256, half * 256 + 256)
        o_ref[512 + half * 256 : 768 + half * 256, :] = (
            v_ref[rows, :].astype(F32) * vs_ref[half, 0].astype(F32)
        ).astype(BF16)
    row = lax.broadcasted_iota(jnp.int32, (META, 128), 0)
    low, high = ks_ref[0, 0].astype(F32), ks_ref[1, 0].astype(F32)
    place = place_ref[0].astype(F32)
    meta = jnp.where(row == 0, low, jnp.where(row == 1, high, jnp.where(row == 2, place, 0.0)))
    o_ref[1024:PAYLOAD, :] = meta.astype(BF16)


def packed(keys, values, k_scale, v_scale, block_place):
    vmem = pl.BlockSpec(memory_space=pltpu.VMEM)
    smem = pl.BlockSpec(memory_space=pltpu.SMEM)
    return pl.pallas_call(
        pack_kernel,
        out_shape=jax.ShapeDtypeStruct((PAYLOAD, 128), BF16),
        in_specs=[vmem, vmem, smem, smem, smem],
        out_specs=vmem,
        name="pack",
    )(keys, values, k_scale.astype(F32), v_scale.astype(F32), block_place)


def group_kernel(inv, sizes, start, finish, *refs):
    refs = list(refs)
    q_ref = refs.pop(0)
    own_ref = refs.pop(0)
    order_ref = refs.pop(0) if finish else None
    others = []
    for size in sizes:
        ref = refs.pop(0)
        others += [(ref, i * PAYLOAD) for i in range(size)]
    if not start:
        del refs[:3]
    att_ref = refs.pop(0) if finish else None
    acc_ref, l_ref, m_ref, kbuf, vbuf, gbuf = refs
    if start:
        own_steps(q_ref, acc_ref, l_ref, m_ref, own_ref, inv)
    own_place = place_of(own_ref)
    other_steps(q_ref, acc_ref, l_ref, m_ref, own_place, others, kbuf, vbuf, gbuf, inv)
    if finish:
        acc_ref[...] = acc_ref[...] / l_ref[...]
        for block in range(8):
            target = pl.ds(pl.multiple_of(order_ref[block] * 64, 64), 64)
            for h in range(8):
                rows = pl.ds(block * 512 + h, 64, stride=8)
                att_ref[target, h * 128 : (h + 1) * 128] = acc_ref[rows, :].astype(BF16)


def attend(q, own, others, state, order, inv, name):
    sizes = [o.shape[0] // PAYLOAD for o in others]
    count = sum(sizes)
    start = state is None
    finish = order is not None
    vmem = pl.BlockSpec(memory_space=pltpu.VMEM)
    shapes = [jax.ShapeDtypeStruct((4096, 128), F32)] * 3
    operands = [q, own] + ([order] if finish else []) + list(others)
    specs = [vmem] * len(operands)
    if finish:
        specs[2] = pl.BlockSpec(memory_space=pltpu.SMEM)
    outs = ([jax.ShapeDtypeStruct((512, 1024), BF16)] if finish else []) + shapes
    aliases = {}
    if not start:
        shift = len(outs) - 3
        aliases = {len(operands) + i: shift + i for i in range(3)}
        operands += list(state)
        specs += [vmem] * 3
    tiles = 2 * count + (3 if start else 0)
    return pl.pallas_call(
        functools.partial(group_kernel, inv, sizes, start, finish),
        out_shape=outs,
        in_specs=specs,
        out_specs=[vmem] * len(outs),
        scratch_shapes=[
            pltpu.VMEM((2 * count * 256, 128), BF16),
            pltpu.VMEM((2 * count * 256, 256), BF16),
            pltpu.VMEM((2 * count, 128), F32),
        ],
        input_output_aliases=aliases,
        compiler_params=pltpu.CompilerParams(vmem_limit_bytes=LIMIT),
        cost_estimate=pl.CostEstimate(
            flops=tiles * 2048 * 256 * 128 * 16,
            transcendentals=tiles * 2048 * 256,
            bytes_accessed=1 << 20,
        ),
        name=name,
    )(*operands)


def project_kernel(blocks, splits, first, columns, a_ref, w_ref, *o_refs):
    rows = jnp.concatenate([a_ref[b * 64 : (b + 1) * 64, :] for b in blocks], axis=0)
    for c in range(0, columns, TILE):
        product = jnp.dot(
            rows, w_ref[:, first + c : first + c + TILE], preferred_element_type=F32
        ).astype(BF16)
        at = 0
        for size, o_ref in zip(splits, o_refs):
            o_ref[:, c : c + TILE] = product[at * 64 : (at + size) * 64, :]
            at += size


def project(att, weight, blocks, splits, first, columns, name):
    vmem = pl.BlockSpec(memory_space=pltpu.VMEM)
    return pl.pallas_call(
        functools.partial(project_kernel, blocks, splits, first, columns),
        out_shape=[jax.ShapeDtypeStruct((s * 64, columns), BF16) for s in splits],
        in_specs=[vmem] * 2,
        out_specs=[vmem] * len(splits),
        compiler_params=pltpu.CompilerParams(vmem_limit_bytes=LIMIT),
        cost_estimate=pl.CostEstimate(
            flops=2 * len(blocks) * 64 * 1024 * columns,
            transcendentals=0,
            bytes_accessed=2 * 1024 * columns,
        ),
        name=name,
    )(att, weight)


def added(*arrays):
    total = arrays[0].astype(F32)
    for a in arrays[1:]:
        total = total + a.astype(F32)
    return total


def scattered(att, weight, first_columns):
    rest = weight.shape[1] - first_columns
    (x_far,) = project(att, weight, (0, 1), (2,), 0, first_columns, "project_far")
    got_far = moved(x_far, ahead)
    (y_out,) = project(att, weight, (1, 3, 5, 7), (4,), first_columns, rest, "project_y")
    got_y = moved(y_out, beside)
    (x_behind,) = project(att, weight, (4, 5), (2,), 0, first_columns, "project_behind")
    got_front = moved(x_behind, behind)
    x_ahead, x_own = project(att, weight, (2, 3, 6, 7), (2, 2), 0, first_columns, "project_c")
    (y_own,) = project(att, weight, (0, 2, 4, 6), (4,), first_columns, rest, "project_d")
    got_back = moved(added(x_ahead, got_far).astype(BF16), ahead)
    y_far, y_ahead, y_behind, y_mine = [
        (y_own[i * 64 : (i + 1) * 64], got_y[i * 64 : (i + 1) * 64]) for i in range(4)
    ]
    x_out = added(x_own[64:], got_front[64:], got_back[64:]).astype(BF16)
    x_last = moved(x_out, beside)
    y_far_sum, y_behind_sum, x_out = lax.optimization_barrier(
        (added(*y_far).astype(BF16), added(*y_behind).astype(BF16), x_out)
    )
    y_got_far = moved(y_far_sum, ahead)
    y_got_front = moved(y_behind_sum, behind)
    y_got_back = moved(added(*y_ahead, y_got_far).astype(BF16), ahead)
    return jnp.concatenate(
        [
            added(x_own[:64], got_front[:64], got_back[:64], x_last).astype(BF16),
            added(*y_mine, y_got_front, y_got_back).astype(BF16),
        ],
        axis=1,
    )


def body(query, keys, values, k_scale, v_scale, block_place, out_weight):
    inv = math.log2(math.e) / math.sqrt(128)
    q = query.reshape(4096, 128)
    k = keys.reshape(512, 128)
    own = packed(k, values.reshape(512, 128), k_scale, v_scale, block_place)
    partner = moved(own, swapped)
    pair = jnp.concatenate([own, partner], axis=0)
    one, two = moved(pair, near), moved(pair, across)
    state = attend(q, own, [partner], None, None, inv, "attend_own")
    pair, four_in, *state = lax.optimization_barrier((pair, own, *state))
    three = moved(pair, diagonal)
    four = moved(four_in, opposite)
    one, two, *state = lax.optimization_barrier((one, two, *state))
    more = moved(jnp.concatenate([one, two], axis=0), swapped)
    state = attend(q, own, [one, two], state, None, inv, "attend_near")
    three, four, *state = lax.optimization_barrier((three, four, *state))
    last = jnp.concatenate([three, four], axis=0)
    final = moved(last, swapped)
    state = attend(q, own, [more], state, None, inv, "attend_more")
    core = lax.axis_index("ctx") % 2
    place = lax.axis_index("head")
    target = jnp.arange(8, dtype=jnp.int32)
    along = (target % 4 - place % 4) % 4
    side = (target // 4 - place // 4) % 2
    forward = 1 + 2 * core
    slot = jnp.where(along == 0, 3, jnp.where(along == 2, 0, jnp.where(along == forward, 1, 2)))
    order = (slot * 2 + side).astype(jnp.int32)
    attended = attend(q, own, [last, final], state, order, inv, "attend_rest")[0]
    return scattered(attended, out_weight, 5120)


def solution(mesh):
    placed = (
        P("ctx", "head", None),
        P("ctx", "head", None),
        P("ctx", "head", None),
        P("ctx", "head"),
        P("ctx", "head"),
        P("ctx"),
        P("head", None),
    )
    return jax.shard_map(
        body, mesh=mesh, in_specs=placed, out_specs=P(("ctx", "head"), None), check_vma=False
    )
```

```python
import functools
import itertools
import math

import jax
import jax.numpy as jnp
from jax import lax
from jax.experimental import pallas as pl
from jax.experimental.pallas import tpu as pltpu
from jax.sharding import PartitionSpec as P

F32 = jnp.float32
BF16 = jnp.bfloat16
AXES = ("ctx", "head")
NEG = -1e30
CHUNK = 128
NT = (((1,), (1,)), ((), ()))
NN = (((1,), (0,)), ((), ()))
META = 16
PAYLOAD = 1024 + META
TILE = 256
LIMIT = 20 << 20


def index_of(z, yh, c, yl, x):
    return ((z % 4) * 4 + (yh % 2) * 2 + c % 2) * 8 + (yl % 2) * 4 + x % 4


def moved(array, target):
    pairs = []
    for at in itertools.product(range(4), range(2), range(2), range(2), range(4)):
        pairs.append((index_of(*at), index_of(*target(*at))))
    return lax.ppermute(array, AXES, pairs)


def swapped(z, yh, c, yl, x):
    return z, yh, 1 - c, yl, x


def near(z, yh, c, yl, x):
    return z + (1 if c == 0 else -1), yh, c, yl, x


def across(z, yh, c, yl, x):
    return (z, yh + 1, c, yl, x) if c == 0 else (z + 2, yh, c, yl, x)


def diagonal(z, yh, c, yl, x):
    return z + (1 if c == 0 else -1), yh + 1, c, yl, x


def opposite(z, yh, c, yl, x):
    return z + 2, yh + 1, c, yl, x


def ahead(z, yh, c, yl, x):
    return z, yh, c, yl, x + (1 if c == 0 else -1)


def behind(z, yh, c, yl, x):
    return z, yh, c, yl, x - (1 if c == 0 else -1)


def beside(z, yh, c, yl, x):
    return z, yh, c, yl + 1, x


def attend_rows(q_ref, acc_ref, l_ref, m_ref, base, count, keys, vals, gains, first=False, visible=None):
    width = keys.shape[0]
    for j in range(count):
        rows = pl.ds(pl.multiple_of(base + j * CHUNK, CHUNK), CHUNK)
        scores = lax.dot_general(q_ref[rows, :], keys, NT, preferred_element_type=F32) * gains
        if visible is not None:
            scores = jnp.where(visible(j), scores, NEG)
        top = jnp.max(scores, axis=1, keepdims=True)
        if first:
            new_m = jnp.broadcast_to(top, (CHUNK, 128))
        else:
            old_m = m_ref[rows, :]
            new_m = jnp.maximum(old_m, top)
        weights = jnp.exp2(scores - jnp.tile(new_m, (1, width // 128)))
        product = lax.dot_general(weights.astype(BF16), vals, NN, preferred_element_type=F32)
        if first:
            acc_ref[rows, :] = product[:, :128]
            l_ref[rows, :] = product[:, 128:]
        else:
            factor = jnp.exp2(old_m - new_m)
            acc_ref[rows, :] = acc_ref[rows, :] * factor + product[:, :128]
            l_ref[rows, :] = l_ref[rows, :] * factor + product[:, 128:]
        m_ref[rows, :] = new_m


def own_steps(q_ref, acc_ref, l_ref, m_ref, own_ref, inv):
    ones = jnp.ones((256, 128), BF16)
    low_k, high_k = own_ref[0:256, :], own_ref[256:512, :]
    low_v = jnp.concatenate([own_ref[512:768, :], ones], axis=1)
    high_v = jnp.concatenate([own_ref[768:1024, :], ones], axis=1)
    low_g = own_ref[1024:1025, :].astype(F32) * inv
    high_g = own_ref[1025:1026, :].astype(F32) * inv

    def low_visible(j):
        token = j * (CHUNK // 8) + lax.broadcasted_iota(jnp.int32, (CHUNK, 256), 0) // 8
        return lax.broadcasted_iota(jnp.int32, (CHUNK, 256), 1) <= token

    def high_visible(j):
        token = 256 + j * (CHUNK // 8) + lax.broadcasted_iota(jnp.int32, (CHUNK, 512), 0) // 8
        return lax.broadcasted_iota(jnp.int32, (CHUNK, 512), 1) <= token

    attend_rows(
        q_ref, acc_ref, l_ref, m_ref, 0, 16, low_k, low_v, jnp.tile(low_g, (1, 2)), True, low_visible
    )
    attend_rows(
        q_ref,
        acc_ref,
        l_ref,
        m_ref,
        2048,
        16,
        jnp.concatenate([low_k, high_k], axis=0),
        jnp.concatenate([low_v, high_v], axis=0),
        jnp.concatenate([low_g, low_g, high_g, high_g], axis=1),
        True,
        high_visible,
    )


def place_of(ref, offset=0):
    return jnp.max(ref[offset + 1026 : offset + 1027, :].astype(F32)).astype(jnp.int32)


def other_steps(q_ref, acc_ref, l_ref, m_ref, own_place, refs, kbuf, vbuf, gbuf, inv):
    count = len(refs)
    vbuf[:, 128:] = jnp.ones((2 * count * 256, 128), BF16)
    highs = jnp.int32(count)
    lows = jnp.int32(0)

    def put(slot, ref, offset, half):
        at = pl.ds(pl.multiple_of(slot * 256, 256), 256)
        source = pl.multiple_of(half * 256, 256)
        kbuf[at, :] = ref[pl.ds(offset + source, 256), :]
        vbuf[at, :128] = ref[pl.ds(offset + 512 + source, 256), :]
        gains = ref[offset + 1024 : offset + 1026, :].astype(F32)
        gbuf[pl.ds(slot, 1), :] = jnp.where(half == 0, gains[0:1], gains[1:2]) * inv

    for i, (ref, offset) in enumerate(refs):
        put(i, ref, offset, 0)
    for ref, offset in refs:
        is_low = (place_of(ref, offset) < own_place).astype(jnp.int32)
        slot = jnp.where(is_low == 1, 2 * count - 1 - lows, highs)
        put(slot, ref, offset, 1 - is_low)
        lows = lows + is_low
        highs = highs + 1 - is_low

    def step(i, carry):
        mixed = 2 * i + 1 == highs

        @pl.when(jnp.logical_not(mixed))
        def _():
            at = pl.multiple_of(i * 512, 512)
            g0 = gbuf[pl.ds(2 * i, 1), :]
            g1 = gbuf[pl.ds(2 * i + 1, 1), :]
            attend_rows(
                q_ref,
                acc_ref,
                l_ref,
                m_ref,
                pl.multiple_of(jnp.where(2 * i + 1 < highs, 2048, 0), 2048),
                16,
                kbuf[pl.ds(at, 512), :],
                vbuf[pl.ds(at, 512), :],
                jnp.concatenate([g0, g0, g1, g1], axis=1),
            )

        @pl.when(mixed)
        def _():
            def single(slot, inner):
                at = pl.multiple_of(slot * 256, 256)
                gain = gbuf[pl.ds(slot, 1), :]
                attend_rows(
                    q_ref,
                    acc_ref,
                    l_ref,
                    m_ref,
                    pl.multiple_of(jnp.where(slot < highs, 2048, 0), 2048),
                    16,
                    kbuf[pl.ds(at, 256), :],
                    vbuf[pl.ds(at, 256), :],
                    jnp.concatenate([gain, gain], axis=1),
                )
                return inner

            lax.fori_loop(2 * i, 2 * i + 2, single, 0)

        return carry

    lax.fori_loop(0, count, step, 0)


def pack_kernel(k_ref, v_ref, ks_ref, vs_ref, place_ref, o_ref):
    o_ref[0:512, :] = k_ref[...]
    for half in range(2):
        rows = slice(half * 256, half * 256 + 256)
        o_ref[512 + half * 256 : 768 + half * 256, :] = (
            v_ref[rows, :].astype(F32) * vs_ref[half : half + 1, :].astype(F32)
        ).astype(BF16)
    row = lax.broadcasted_iota(jnp.int32, (META, 128), 0)
    low, high = ks_ref[0:1, :].astype(F32), ks_ref[1:2, :].astype(F32)
    place = place_ref[0].astype(F32)
    meta = jnp.where(row == 0, low, jnp.where(row == 1, high, jnp.where(row == 2, place, 0.0)))
    o_ref[1024:PAYLOAD, :] = meta.astype(BF16)


def packed(keys, values, k_scale, v_scale, block_place):
    vmem = pl.BlockSpec(memory_space=pltpu.VMEM)
    smem = pl.BlockSpec(memory_space=pltpu.SMEM)
    return pl.pallas_call(
        pack_kernel,
        out_shape=jax.ShapeDtypeStruct((PAYLOAD, 128), BF16),
        in_specs=[vmem, vmem, vmem, vmem, smem],
        out_specs=vmem,
        name="pack",
    )(keys, values, k_scale, v_scale, block_place)


def group_kernel(inv, sizes, start, finish, *refs):
    refs = list(refs)
    q_ref = refs.pop(0)
    own_ref = refs.pop(0)
    order_ref = refs.pop(0) if finish else None
    others = []
    for size in sizes:
        ref = refs.pop(0)
        others += [(ref, i * PAYLOAD) for i in range(size)]
    if not start:
        del refs[:3]
    att_ref = refs.pop(0) if finish else None
    acc_ref, l_ref, m_ref, kbuf, vbuf, gbuf = refs
    if start:
        own_steps(q_ref, acc_ref, l_ref, m_ref, own_ref, inv)
    own_place = place_of(own_ref)
    if others:
        other_steps(
            q_ref, acc_ref, l_ref, m_ref, own_place, others, kbuf, vbuf, gbuf, inv
        )
    if finish:
        acc_ref[...] = acc_ref[...] / l_ref[...]
        for block in range(8):
            target = pl.ds(pl.multiple_of(order_ref[block] * 64, 64), 64)
            for h in range(8):
                rows = pl.ds(block * 512 + h, 64, stride=8)
                att_ref[target, h * 128 : (h + 1) * 128] = acc_ref[rows, :].astype(BF16)


def attend(q, own, others, state, order, inv, name):
    sizes = [o.shape[0] // PAYLOAD for o in others]
    count = sum(sizes)
    start = state is None
    finish = order is not None
    vmem = pl.BlockSpec(memory_space=pltpu.VMEM)
    shapes = [jax.ShapeDtypeStruct((4096, 128), F32)] * 3
    operands = [q, own] + ([order] if finish else []) + list(others)
    specs = [vmem] * len(operands)
    if finish:
        specs[2] = pl.BlockSpec(memory_space=pltpu.SMEM)
    outs = ([jax.ShapeDtypeStruct((512, 1024), BF16)] if finish else []) + shapes
    aliases = {}
    if not start:
        shift = len(outs) - 3
        aliases = {len(operands) + i: shift + i for i in range(3)}
        operands += list(state)
        specs += [vmem] * 3
    tiles = 2 * count + (3 if start else 0)
    return pl.pallas_call(
        functools.partial(group_kernel, inv, sizes, start, finish),
        out_shape=outs,
        in_specs=specs,
        out_specs=[vmem] * len(outs),
        scratch_shapes=[
            pltpu.VMEM((max(count, 1) * 512, 128), BF16),
            pltpu.VMEM((max(count, 1) * 512, 256), BF16),
            pltpu.VMEM((max(count, 1) * 2, 128), F32),
        ],
        input_output_aliases=aliases,
        compiler_params=pltpu.CompilerParams(vmem_limit_bytes=LIMIT),
        cost_estimate=pl.CostEstimate(
            flops=tiles * 2048 * 256 * 128 * 16,
            transcendentals=tiles * 2048 * 256,
            bytes_accessed=1 << 20,
        ),
        name=name,
    )(*operands)


def project_kernel(blocks, splits, first, columns, a_ref, w_ref, *o_refs):
    rows = jnp.concatenate([a_ref[b * 64 : (b + 1) * 64, :] for b in blocks], axis=0)
    for c in range(0, columns, TILE):
        product = jnp.dot(
            rows, w_ref[:, first + c : first + c + TILE], preferred_element_type=F32
        ).astype(BF16)
        at = 0
        for size, o_ref in zip(splits, o_refs):
            o_ref[:, c : c + TILE] = product[at * 64 : (at + size) * 64, :]
            at += size


def project(att, weight, blocks, splits, first, columns, name):
    vmem = pl.BlockSpec(memory_space=pltpu.VMEM)
    return pl.pallas_call(
        functools.partial(project_kernel, blocks, splits, first, columns),
        out_shape=[jax.ShapeDtypeStruct((s * 64, columns), BF16) for s in splits],
        in_specs=[vmem] * 2,
        out_specs=[vmem] * len(splits),
        compiler_params=pltpu.CompilerParams(vmem_limit_bytes=LIMIT),
        cost_estimate=pl.CostEstimate(
            flops=2 * len(blocks) * 64 * 1024 * columns,
            transcendentals=0,
            bytes_accessed=2 * 1024 * columns,
        ),
        name=name,
    )(att, weight)


def added(*arrays):
    total = arrays[0].astype(F32)
    for a in arrays[1:]:
        total = total + a.astype(F32)
    return total


def scattered(att, weight, first_columns):
    rest = weight.shape[1] - first_columns
    (x_far,) = project(att, weight, (0, 1), (2,), 0, first_columns, "project_far")
    got_far = moved(x_far, ahead)
    (y_out,) = project(att, weight, (1, 3, 5, 7), (4,), first_columns, rest, "project_y")
    got_y = moved(y_out, beside)
    att, x_far, y_out = lax.optimization_barrier((att, x_far, y_out))
    (x_behind,) = project(att, weight, (4, 5), (2,), 0, first_columns, "project_behind")
    got_front = moved(x_behind, behind)
    att, x_behind = lax.optimization_barrier((att, x_behind))
    x_ahead, x_own = project(att, weight, (2, 3, 6, 7), (2, 2), 0, first_columns, "project_c")
    (y_own,) = project(att, weight, (0, 2, 4, 6), (4,), first_columns, rest, "project_d")
    got_back = moved(added(x_ahead, got_far).astype(BF16), ahead)
    y_far, y_ahead, y_behind, y_mine = [
        (y_own[i * 64 : (i + 1) * 64], got_y[i * 64 : (i + 1) * 64]) for i in range(4)
    ]
    x_out = added(x_own[64:], got_front[64:], got_back[64:]).astype(BF16)
    x_last = moved(x_out, beside)
    y_far_sum, y_behind_sum, x_out = lax.optimization_barrier(
        (added(*y_far).astype(BF16), added(*y_behind).astype(BF16), x_out)
    )
    y_got_far = moved(y_far_sum, ahead)
    y_got_front = moved(y_behind_sum, behind)
    y_got_back = moved(added(*y_ahead, y_got_far).astype(BF16), ahead)
    return jnp.concatenate(
        [
            added(x_own[:64], got_front[:64], got_back[:64], x_last).astype(BF16),
            added(*y_mine, y_got_front, y_got_back).astype(BF16),
        ],
        axis=1,
    )


def body(query, keys, values, k_scale, v_scale, block_place, out_weight):
    inv = math.log2(math.e) / math.sqrt(128)
    q = query.reshape(4096, 128)
    k = keys.reshape(512, 128)
    own = packed(k, values.reshape(512, 128), k_scale, v_scale, block_place)
    core = lax.axis_index("ctx") % 2
    place = lax.axis_index("head")
    target = jnp.arange(8, dtype=jnp.int32)
    along = (target % 4 - place % 4) % 4
    side = (target // 4 - place // 4) % 2
    forward = 1 + 2 * core
    slot = jnp.where(along == 0, 3, jnp.where(along == 2, 0, jnp.where(along == forward, 1, 2)))
    order = (slot * 2 + side).astype(jnp.int32)
    own, order = lax.optimization_barrier((own, order))
    partner = moved(own, swapped)
    pair = jnp.concatenate([own, partner], axis=0)
    one, two = moved(pair, near), moved(pair, across)
    state = attend(q, own, [], None, None, inv, "attend_own")
    pair, mine, *state = lax.optimization_barrier((pair, own, *state))
    three, four = moved(pair, diagonal), moved(mine, opposite)
    state = attend(q, own, [partner], state, None, inv, "attend_partner")
    one, two, *state = lax.optimization_barrier((one, two, *state))
    more = moved(jnp.concatenate([one, two], axis=0), swapped)
    state = attend(q, own, [one, two], state, None, inv, "attend_near")
    state = attend(q, own, [more], state, None, inv, "attend_more")
    three, four, *state = lax.optimization_barrier((three, four, *state))
    last = jnp.concatenate([three, four], axis=0)
    final = moved(last, swapped)
    state = attend(q, own, [last], state, None, inv, "attend_last")
    attended = attend(q, own, [final], state, order, inv, "attend_rest")[0]
    return scattered(attended, out_weight, 4864)


def solution(mesh):
    placed = (
        P("ctx", "head", None),
        P("ctx", "head", None),
        P("ctx", "head", None),
        P("ctx", "head"),
        P("ctx", "head"),
        P("ctx"),
        P("head", None),
    )
    return jax.shard_map(
        body, mesh=mesh, in_specs=placed, out_specs=P(("ctx", "head"), None), check_vma=False
    )
```

```python
import functools
import itertools
import math

import jax
import jax.numpy as jnp
from jax import lax
from jax.experimental import pallas as pl
from jax.experimental.pallas import tpu as pltpu
from jax.sharding import PartitionSpec as P

F32 = jnp.float32
BF16 = jnp.bfloat16
AXES = ("ctx", "head")
NEG = -1e30
CHUNK = 128
NT = (((1,), (1,)), ((), ()))
NN = (((1,), (0,)), ((), ()))
META = 16
PAYLOAD = 1024 + META
TILE = 256
LIMIT = 20 << 20


def index_of(z, yh, c, yl, x):
    return ((z % 4) * 4 + (yh % 2) * 2 + c % 2) * 8 + (yl % 2) * 4 + x % 4


def moved(array, target):
    pairs = []
    for at in itertools.product(range(4), range(2), range(2), range(2), range(4)):
        pairs.append((index_of(*at), index_of(*target(*at))))
    return lax.ppermute(array, AXES, pairs)


def swapped(z, yh, c, yl, x):
    return z, yh, 1 - c, yl, x


def near(z, yh, c, yl, x):
    return z + (1 if c == 0 else -1), yh, c, yl, x


def across(z, yh, c, yl, x):
    return (z, yh + 1, c, yl, x) if c == 0 else (z + 2, yh, c, yl, x)


def diagonal(z, yh, c, yl, x):
    return z + (1 if c == 0 else -1), yh + 1, c, yl, x


def opposite(z, yh, c, yl, x):
    return z + 2, yh + 1, c, yl, x


def ahead(z, yh, c, yl, x):
    return z, yh, c, yl, x + (1 if c == 0 else -1)


def behind(z, yh, c, yl, x):
    return z, yh, c, yl, x - (1 if c == 0 else -1)


def beside(z, yh, c, yl, x):
    return z, yh, c, yl + 1, x


def attend_rows(q_ref, acc_ref, l_ref, m_ref, base, count, keys, vals, gains, first=False, visible=None):
    width = keys.shape[0]
    for j in range(count):
        rows = pl.ds(pl.multiple_of(base + j * CHUNK, CHUNK), CHUNK)
        scores = lax.dot_general(q_ref[rows, :], keys, NT, preferred_element_type=F32) * gains
        if visible is not None:
            scores = jnp.where(visible(j), scores, NEG)
        top = jnp.max(scores, axis=1, keepdims=True)
        if first:
            new_m = jnp.broadcast_to(top, (CHUNK, 128))
        else:
            old_m = m_ref[rows, :]
            new_m = jnp.maximum(old_m, top)
        weights = jnp.exp2(scores - jnp.tile(new_m, (1, width // 128)))
        product = lax.dot_general(weights.astype(BF16), vals, NN, preferred_element_type=F32)
        if first:
            acc_ref[rows, :] = product[:, :128]
            l_ref[rows, :] = product[:, 128:]
        else:
            factor = jnp.exp2(old_m - new_m)
            acc_ref[rows, :] = acc_ref[rows, :] * factor + product[:, :128]
            l_ref[rows, :] = l_ref[rows, :] * factor + product[:, 128:]
        m_ref[rows, :] = new_m


def own_steps(q_ref, acc_ref, l_ref, m_ref, own_ref, inv):
    ones = jnp.ones((256, 128), BF16)
    low_k, high_k = own_ref[0:256, :], own_ref[256:512, :]
    low_v = jnp.concatenate([own_ref[512:768, :], ones], axis=1)
    high_v = jnp.concatenate([own_ref[768:1024, :], ones], axis=1)
    low_g = own_ref[1024:1025, :].astype(F32) * inv
    high_g = own_ref[1025:1026, :].astype(F32) * inv

    def low_visible(j):
        token = j * (CHUNK // 8) + lax.broadcasted_iota(jnp.int32, (CHUNK, 256), 0) // 8
        return lax.broadcasted_iota(jnp.int32, (CHUNK, 256), 1) <= token

    def high_visible(j):
        token = 256 + j * (CHUNK // 8) + lax.broadcasted_iota(jnp.int32, (CHUNK, 512), 0) // 8
        return lax.broadcasted_iota(jnp.int32, (CHUNK, 512), 1) <= token

    attend_rows(
        q_ref, acc_ref, l_ref, m_ref, 0, 16, low_k, low_v, jnp.tile(low_g, (1, 2)), True, low_visible
    )
    attend_rows(
        q_ref,
        acc_ref,
        l_ref,
        m_ref,
        2048,
        16,
        jnp.concatenate([low_k, high_k], axis=0),
        jnp.concatenate([low_v, high_v], axis=0),
        jnp.concatenate([low_g, low_g, high_g, high_g], axis=1),
        True,
        high_visible,
    )


def place_of(ref, offset=0):
    return jnp.max(ref[offset + 1026 : offset + 1027, :].astype(F32)).astype(jnp.int32)


def other_steps(q_ref, acc_ref, l_ref, m_ref, own_place, refs, kbuf, vbuf, gbuf, inv):
    count = len(refs)
    vbuf[:, 128:] = jnp.ones((2 * count * 256, 128), BF16)
    highs = jnp.int32(count)
    lows = jnp.int32(0)

    def put(slot, ref, offset, half):
        at = pl.ds(pl.multiple_of(slot * 256, 256), 256)
        source = pl.multiple_of(half * 256, 256)
        kbuf[at, :] = ref[pl.ds(offset + source, 256), :]
        vbuf[at, :128] = ref[pl.ds(offset + 512 + source, 256), :]
        gains = ref[offset + 1024 : offset + 1026, :].astype(F32)
        gbuf[pl.ds(slot, 1), :] = jnp.where(half == 0, gains[0:1], gains[1:2]) * inv

    for i, (ref, offset) in enumerate(refs):
        put(i, ref, offset, 0)
    for ref, offset in refs:
        is_low = (place_of(ref, offset) < own_place).astype(jnp.int32)
        slot = jnp.where(is_low == 1, 2 * count - 1 - lows, highs)
        put(slot, ref, offset, 1 - is_low)
        lows = lows + is_low
        highs = highs + 1 - is_low

    def step(i, carry):
        mixed = 2 * i + 1 == highs

        @pl.when(jnp.logical_not(mixed))
        def _():
            at = pl.multiple_of(i * 512, 512)
            g0 = gbuf[pl.ds(2 * i, 1), :]
            g1 = gbuf[pl.ds(2 * i + 1, 1), :]
            attend_rows(
                q_ref,
                acc_ref,
                l_ref,
                m_ref,
                pl.multiple_of(jnp.where(2 * i + 1 < highs, 2048, 0), 2048),
                16,
                kbuf[pl.ds(at, 512), :],
                vbuf[pl.ds(at, 512), :],
                jnp.concatenate([g0, g0, g1, g1], axis=1),
            )

        @pl.when(mixed)
        def _():
            def single(slot, inner):
                at = pl.multiple_of(slot * 256, 256)
                gain = gbuf[pl.ds(slot, 1), :]
                attend_rows(
                    q_ref,
                    acc_ref,
                    l_ref,
                    m_ref,
                    pl.multiple_of(jnp.where(slot < highs, 2048, 0), 2048),
                    16,
                    kbuf[pl.ds(at, 256), :],
                    vbuf[pl.ds(at, 256), :],
                    jnp.concatenate([gain, gain], axis=1),
                )
                return inner

            lax.fori_loop(2 * i, 2 * i + 2, single, 0)

        return carry

    lax.fori_loop(0, count, step, 0)


def pack_kernel(k_ref, v_ref, ks_ref, vs_ref, place_ref, o_ref):
    o_ref[0:512, :] = k_ref[...]
    for half in range(2):
        rows = slice(half * 256, half * 256 + 256)
        o_ref[512 + half * 256 : 768 + half * 256, :] = (
            v_ref[rows, :].astype(F32) * vs_ref[half : half + 1, :].astype(F32)
        ).astype(BF16)
    row = lax.broadcasted_iota(jnp.int32, (META, 128), 0)
    low, high = ks_ref[0:1, :].astype(F32), ks_ref[1:2, :].astype(F32)
    place = place_ref[0].astype(F32)
    meta = jnp.where(row == 0, low, jnp.where(row == 1, high, jnp.where(row == 2, place, 0.0)))
    o_ref[1024:PAYLOAD, :] = meta.astype(BF16)


def packed(keys, values, k_scale, v_scale, block_place):
    vmem = pl.BlockSpec(memory_space=pltpu.VMEM)
    smem = pl.BlockSpec(memory_space=pltpu.SMEM)
    return pl.pallas_call(
        pack_kernel,
        out_shape=jax.ShapeDtypeStruct((PAYLOAD, 128), BF16),
        in_specs=[vmem, vmem, vmem, vmem, smem],
        out_specs=vmem,
        name="pack",
    )(keys, values, k_scale, v_scale, block_place)


def group_kernel(inv, sizes, start, finish, *refs):
    refs = list(refs)
    q_ref = refs.pop(0)
    own_ref = refs.pop(0)
    order_ref = refs.pop(0) if finish else None
    others = []
    for size in sizes:
        ref = refs.pop(0)
        others += [(ref, i * PAYLOAD) for i in range(size)]
    if not start:
        del refs[:3]
    att_ref = refs.pop(0) if finish else None
    acc_ref, l_ref, m_ref, kbuf, vbuf, gbuf = refs
    if start:
        own_steps(q_ref, acc_ref, l_ref, m_ref, own_ref, inv)
    own_place = place_of(own_ref)
    if others:
        other_steps(
            q_ref, acc_ref, l_ref, m_ref, own_place, others, kbuf, vbuf, gbuf, inv
        )
    if finish:
        acc_ref[...] = acc_ref[...] / l_ref[...]
        for block in range(8):
            target = pl.ds(pl.multiple_of(order_ref[block] * 64, 64), 64)
            for h in range(8):
                rows = pl.ds(block * 512 + h, 64, stride=8)
                att_ref[target, h * 128 : (h + 1) * 128] = acc_ref[rows, :].astype(BF16)


def attend(q, own, others, state, order, inv, name):
    sizes = [o.shape[0] // PAYLOAD for o in others]
    count = sum(sizes)
    start = state is None
    finish = order is not None
    vmem = pl.BlockSpec(memory_space=pltpu.VMEM)
    shapes = [jax.ShapeDtypeStruct((4096, 128), F32)] * 3
    operands = [q, own] + ([order] if finish else []) + list(others)
    specs = [vmem] * len(operands)
    if finish:
        specs[2] = pl.BlockSpec(memory_space=pltpu.SMEM)
    outs = ([jax.ShapeDtypeStruct((512, 1024), BF16)] if finish else []) + shapes
    aliases = {}
    if not start:
        shift = len(outs) - 3
        aliases = {len(operands) + i: shift + i for i in range(3)}
        operands += list(state)
        specs += [vmem] * 3
    tiles = 2 * count + (3 if start else 0)
    return pl.pallas_call(
        functools.partial(group_kernel, inv, sizes, start, finish),
        out_shape=outs,
        in_specs=specs,
        out_specs=[vmem] * len(outs),
        scratch_shapes=[
            pltpu.VMEM((max(count, 1) * 512, 128), BF16),
            pltpu.VMEM((max(count, 1) * 512, 256), BF16),
            pltpu.VMEM((max(count, 1) * 2, 128), F32),
        ],
        input_output_aliases=aliases,
        compiler_params=pltpu.CompilerParams(vmem_limit_bytes=LIMIT),
        cost_estimate=pl.CostEstimate(
            flops=tiles * 2048 * 256 * 128 * 16,
            transcendentals=tiles * 2048 * 256,
            bytes_accessed=1 << 20,
        ),
        name=name,
    )(*operands)


def project_kernel(blocks, splits, first, columns, a_ref, w_ref, *o_refs):
    rows = jnp.concatenate([a_ref[b * 64 : (b + 1) * 64, :] for b in blocks], axis=0)
    for c in range(0, columns, TILE):
        product = jnp.dot(
            rows, w_ref[:, first + c : first + c + TILE], preferred_element_type=F32
        ).astype(BF16)
        at = 0
        for size, o_ref in zip(splits, o_refs):
            o_ref[:, c : c + TILE] = product[at * 64 : (at + size) * 64, :]
            at += size


def project(att, weight, blocks, splits, first, columns, name):
    vmem = pl.BlockSpec(memory_space=pltpu.VMEM)
    return pl.pallas_call(
        functools.partial(project_kernel, blocks, splits, first, columns),
        out_shape=[jax.ShapeDtypeStruct((s * 64, columns), BF16) for s in splits],
        in_specs=[vmem] * 2,
        out_specs=[vmem] * len(splits),
        compiler_params=pltpu.CompilerParams(vmem_limit_bytes=LIMIT),
        cost_estimate=pl.CostEstimate(
            flops=2 * len(blocks) * 64 * 1024 * columns,
            transcendentals=0,
            bytes_accessed=2 * 1024 * columns,
        ),
        name=name,
    )(att, weight)


def added(*arrays):
    total = arrays[0].astype(F32)
    for a in arrays[1:]:
        total = total + a.astype(F32)
    return total


def scattered(att, weight, first_columns):
    rest = weight.shape[1] - first_columns
    (x_far,) = project(att, weight, (0, 1), (2,), 0, first_columns, "project_far")
    got_far = moved(x_far, ahead)
    (y_out,) = project(att, weight, (1, 3, 5, 7), (4,), first_columns, rest, "project_y")
    got_y = moved(y_out, beside)
    att, x_far, y_out = lax.optimization_barrier((att, x_far, y_out))
    x_ahead, x_own = project(att, weight, (2, 3, 6, 7), (2, 2), 0, first_columns, "project_c")
    att, x_ahead, x_own = lax.optimization_barrier((att, x_ahead, x_own))
    (x_behind,) = project(att, weight, (4, 5), (2,), 0, first_columns, "project_behind")
    got_front = moved(x_behind, behind)
    att, x_behind = lax.optimization_barrier((att, x_behind))
    (y_own,) = project(att, weight, (0, 2, 4, 6), (4,), first_columns, rest, "project_d")
    got_back = moved(added(x_ahead, got_far).astype(BF16), ahead)
    y_far, y_ahead, y_behind, y_mine = [
        (y_own[i * 64 : (i + 1) * 64], got_y[i * 64 : (i + 1) * 64]) for i in range(4)
    ]
    x_out = added(x_own[64:], got_front[64:], got_back[64:]).astype(BF16)
    x_last = moved(x_out, beside)
    y_far_sum, y_behind_sum, x_out = lax.optimization_barrier(
        (added(*y_far).astype(BF16), added(*y_behind).astype(BF16), x_out)
    )
    y_got_far = moved(y_far_sum, ahead)
    y_got_front = moved(y_behind_sum, behind)
    y_got_back = moved(added(*y_ahead, y_got_far).astype(BF16), ahead)
    return jnp.concatenate(
        [
            added(x_own[:64], got_front[:64], got_back[:64], x_last).astype(BF16),
            added(*y_mine, y_got_front, y_got_back).astype(BF16),
        ],
        axis=1,
    )


def body(query, keys, values, k_scale, v_scale, block_place, out_weight):
    inv = math.log2(math.e) / math.sqrt(128)
    q = query.reshape(4096, 128)
    k = keys.reshape(512, 128)
    own = packed(k, values.reshape(512, 128), k_scale, v_scale, block_place)
    core = lax.axis_index("ctx") % 2
    place = lax.axis_index("head")
    target = jnp.arange(8, dtype=jnp.int32)
    along = (target % 4 - place % 4) % 4
    side = (target // 4 - place // 4) % 2
    forward = 1 + 2 * core
    slot = jnp.where(along == 0, 3, jnp.where(along == 2, 0, jnp.where(along == forward, 1, 2)))
    order = (slot * 2 + side).astype(jnp.int32)
    own, order = lax.optimization_barrier((own, order))
    partner = moved(own, swapped)
    pair = jnp.concatenate([own, partner], axis=0)
    one, two = moved(pair, near), moved(pair, across)
    state = attend(q, own, [], None, None, inv, "attend_own")
    pair, mine, *state = lax.optimization_barrier((pair, own, *state))
    three, four = moved(pair, diagonal), moved(mine, opposite)
    state = attend(q, own, [partner], state, None, inv, "attend_partner")
    one, two, *state = lax.optimization_barrier((one, two, *state))
    more = moved(jnp.concatenate([one, two], axis=0), swapped)
    state = attend(q, own, [one, two], state, None, inv, "attend_near")
    state = attend(q, own, [more], state, None, inv, "attend_more")
    three, four, *state = lax.optimization_barrier((three, four, *state))
    last = jnp.concatenate([three, four], axis=0)
    final = moved(last, swapped)
    state = attend(q, own, [last], state, None, inv, "attend_last")
    attended = attend(q, own, [final], state, order, inv, "attend_rest")[0]
    return scattered(attended, out_weight, 4864)


def solution(mesh):
    placed = (
        P("ctx", "head", None),
        P("ctx", "head", None),
        P("ctx", "head", None),
        P("ctx", "head"),
        P("ctx", "head"),
        P("ctx"),
        P("head", None),
    )
    return jax.shard_map(
        body, mesh=mesh, in_specs=placed, out_specs=P(("ctx", "head"), None), check_vma=False
    )
```

```python
import functools
import itertools
import math

import jax
import jax.numpy as jnp
from jax import lax
from jax.experimental import pallas as pl
from jax.experimental.pallas import tpu as pltpu
from jax.sharding import PartitionSpec as P

F32 = jnp.float32
BF16 = jnp.bfloat16
AXES = ("ctx", "head")
NEG = -1e30
CHUNK = 128
NT = (((1,), (1,)), ((), ()))
NN = (((1,), (0,)), ((), ()))
META = 16
PAYLOAD = 1024 + META
TILE = 256
LIMIT = 20 << 20


def index_of(z, yh, c, yl, x):
    return ((z % 4) * 4 + (yh % 2) * 2 + c % 2) * 8 + (yl % 2) * 4 + x % 4


def moved(array, target):
    pairs = []
    for at in itertools.product(range(4), range(2), range(2), range(2), range(4)):
        pairs.append((index_of(*at), index_of(*target(*at))))
    return lax.ppermute(array, AXES, pairs)


def swapped(z, yh, c, yl, x):
    return z, yh, 1 - c, yl, x


def near(z, yh, c, yl, x):
    return z + (1 if c == 0 else -1), yh, c, yl, x


def across(z, yh, c, yl, x):
    return (z, yh + 1, c, yl, x) if c == 0 else (z + 2, yh, c, yl, x)


def diagonal(z, yh, c, yl, x):
    return z + (1 if c == 0 else -1), yh + 1, c, yl, x


def opposite(z, yh, c, yl, x):
    return z + 2, yh + 1, c, yl, x


def ahead(z, yh, c, yl, x):
    return z, yh, c, yl, x + (1 if c == 0 else -1)


def behind(z, yh, c, yl, x):
    return z, yh, c, yl, x - (1 if c == 0 else -1)


def beside(z, yh, c, yl, x):
    return z, yh, c, yl + 1, x


def attend_rows(q_ref, acc_ref, l_ref, m_ref, base, count, keys, vals, gains, first=False, visible=None):
    width = keys.shape[0]
    for j in range(count):
        rows = pl.ds(pl.multiple_of(base + j * CHUNK, CHUNK), CHUNK)
        scores = lax.dot_general(q_ref[rows, :], keys, NT, preferred_element_type=F32) * gains
        if visible is not None:
            scores = jnp.where(visible(j), scores, NEG)
        top = jnp.max(scores, axis=1, keepdims=True)
        if first:
            new_m = jnp.broadcast_to(top, (CHUNK, 128))
        else:
            old_m = m_ref[rows, :]
            new_m = jnp.maximum(old_m, top)
        weights = jnp.exp2(scores - jnp.tile(new_m, (1, width // 128)))
        product = lax.dot_general(weights.astype(BF16), vals, NN, preferred_element_type=F32)
        if first:
            acc_ref[rows, :] = product[:, :128]
            l_ref[rows, :] = product[:, 128:]
        else:
            factor = jnp.exp2(old_m - new_m)
            acc_ref[rows, :] = acc_ref[rows, :] * factor + product[:, :128]
            l_ref[rows, :] = l_ref[rows, :] * factor + product[:, 128:]
        m_ref[rows, :] = new_m


def own_steps(q_ref, acc_ref, l_ref, m_ref, own_ref, inv):
    ones = jnp.ones((256, 128), BF16)
    low_k, high_k = own_ref[0:256, :], own_ref[256:512, :]
    low_v = jnp.concatenate([own_ref[512:768, :], ones], axis=1)
    high_v = jnp.concatenate([own_ref[768:1024, :], ones], axis=1)
    low_g = own_ref[1024:1025, :].astype(F32) * inv
    high_g = own_ref[1025:1026, :].astype(F32) * inv

    def low_visible(j):
        token = j * (CHUNK // 8) + lax.broadcasted_iota(jnp.int32, (CHUNK, 256), 0) // 8
        return lax.broadcasted_iota(jnp.int32, (CHUNK, 256), 1) <= token

    def high_visible(j):
        token = 256 + j * (CHUNK // 8) + lax.broadcasted_iota(jnp.int32, (CHUNK, 512), 0) // 8
        return lax.broadcasted_iota(jnp.int32, (CHUNK, 512), 1) <= token

    attend_rows(
        q_ref, acc_ref, l_ref, m_ref, 0, 16, low_k, low_v, jnp.tile(low_g, (1, 2)), True, low_visible
    )
    attend_rows(
        q_ref,
        acc_ref,
        l_ref,
        m_ref,
        2048,
        16,
        jnp.concatenate([low_k, high_k], axis=0),
        jnp.concatenate([low_v, high_v], axis=0),
        jnp.concatenate([low_g, low_g, high_g, high_g], axis=1),
        True,
        high_visible,
    )


def place_of(ref, offset=0):
    return jnp.max(ref[offset + 1026 : offset + 1027, :].astype(F32)).astype(jnp.int32)


def other_steps(q_ref, acc_ref, l_ref, m_ref, own_place, refs, kbuf, vbuf, gbuf, inv):
    count = len(refs)
    vbuf[:, 128:] = jnp.ones((2 * count * 256, 128), BF16)
    highs = jnp.int32(count)
    lows = jnp.int32(0)

    def put(slot, ref, offset, half):
        at = pl.ds(pl.multiple_of(slot * 256, 256), 256)
        source = pl.multiple_of(half * 256, 256)
        kbuf[at, :] = ref[pl.ds(offset + source, 256), :]
        vbuf[at, :128] = ref[pl.ds(offset + 512 + source, 256), :]
        gains = ref[offset + 1024 : offset + 1026, :].astype(F32)
        gbuf[pl.ds(slot, 1), :] = jnp.where(half == 0, gains[0:1], gains[1:2]) * inv

    for i, (ref, offset) in enumerate(refs):
        put(i, ref, offset, 0)
    for ref, offset in refs:
        is_low = (place_of(ref, offset) < own_place).astype(jnp.int32)
        slot = jnp.where(is_low == 1, 2 * count - 1 - lows, highs)
        put(slot, ref, offset, 1 - is_low)
        lows = lows + is_low
        highs = highs + 1 - is_low

    def step(i, carry):
        mixed = 2 * i + 1 == highs

        @pl.when(jnp.logical_not(mixed))
        def _():
            at = pl.multiple_of(i * 512, 512)
            g0 = gbuf[pl.ds(2 * i, 1), :]
            g1 = gbuf[pl.ds(2 * i + 1, 1), :]
            attend_rows(
                q_ref,
                acc_ref,
                l_ref,
                m_ref,
                pl.multiple_of(jnp.where(2 * i + 1 < highs, 2048, 0), 2048),
                16,
                kbuf[pl.ds(at, 512), :],
                vbuf[pl.ds(at, 512), :],
                jnp.concatenate([g0, g0, g1, g1], axis=1),
            )

        @pl.when(mixed)
        def _():
            def single(slot, inner):
                at = pl.multiple_of(slot * 256, 256)
                gain = gbuf[pl.ds(slot, 1), :]
                attend_rows(
                    q_ref,
                    acc_ref,
                    l_ref,
                    m_ref,
                    pl.multiple_of(jnp.where(slot < highs, 2048, 0), 2048),
                    16,
                    kbuf[pl.ds(at, 256), :],
                    vbuf[pl.ds(at, 256), :],
                    jnp.concatenate([gain, gain], axis=1),
                )
                return inner

            lax.fori_loop(2 * i, 2 * i + 2, single, 0)

        return carry

    lax.fori_loop(0, count, step, 0)


def pack_kernel(k_ref, v_ref, ks_ref, vs_ref, place_ref, o_ref):
    o_ref[0:512, :] = k_ref[...]
    for half in range(2):
        rows = slice(half * 256, half * 256 + 256)
        o_ref[512 + half * 256 : 768 + half * 256, :] = (
            v_ref[rows, :].astype(F32) * vs_ref[half : half + 1, :].astype(F32)
        ).astype(BF16)
    row = lax.broadcasted_iota(jnp.int32, (META, 128), 0)
    low, high = ks_ref[0:1, :].astype(F32), ks_ref[1:2, :].astype(F32)
    place = place_ref[0].astype(F32)
    meta = jnp.where(row == 0, low, jnp.where(row == 1, high, jnp.where(row == 2, place, 0.0)))
    o_ref[1024:PAYLOAD, :] = meta.astype(BF16)


def packed(keys, values, k_scale, v_scale, block_place):
    vmem = pl.BlockSpec(memory_space=pltpu.VMEM)
    smem = pl.BlockSpec(memory_space=pltpu.SMEM)
    return pl.pallas_call(
        pack_kernel,
        out_shape=jax.ShapeDtypeStruct((PAYLOAD, 128), BF16),
        in_specs=[vmem, vmem, vmem, vmem, smem],
        out_specs=vmem,
        name="pack",
    )(keys, values, k_scale, v_scale, block_place)


def group_kernel(inv, sizes, start, finish, *refs):
    refs = list(refs)
    q_ref = refs.pop(0)
    own_ref = refs.pop(0)
    order_ref = refs.pop(0) if finish else None
    others = []
    for size in sizes:
        ref = refs.pop(0)
        others += [(ref, i * PAYLOAD) for i in range(size)]
    if not start:
        del refs[:3]
    att_ref = refs.pop(0) if finish else None
    acc_ref, l_ref, m_ref, kbuf, vbuf, gbuf = refs
    if start:
        own_steps(q_ref, acc_ref, l_ref, m_ref, own_ref, inv)
    own_place = place_of(own_ref)
    if others:
        other_steps(
            q_ref, acc_ref, l_ref, m_ref, own_place, others, kbuf, vbuf, gbuf, inv
        )
    if finish:
        acc_ref[...] = acc_ref[...] / l_ref[...]
        for block in range(8):
            target = pl.ds(pl.multiple_of(order_ref[block] * 64, 64), 64)
            for h in range(8):
                rows = pl.ds(block * 512 + h, 64, stride=8)
                att_ref[target, h * 128 : (h + 1) * 128] = acc_ref[rows, :].astype(BF16)


def attend(q, own, others, state, order, inv, name):
    sizes = [o.shape[0] // PAYLOAD for o in others]
    count = sum(sizes)
    start = state is None
    finish = order is not None
    vmem = pl.BlockSpec(memory_space=pltpu.VMEM)
    shapes = [jax.ShapeDtypeStruct((4096, 128), F32)] * 3
    operands = [q, own] + ([order] if finish else []) + list(others)
    specs = [vmem] * len(operands)
    if finish:
        specs[2] = pl.BlockSpec(memory_space=pltpu.SMEM)
    outs = ([jax.ShapeDtypeStruct((512, 1024), BF16)] if finish else []) + shapes
    aliases = {}
    if not start:
        shift = len(outs) - 3
        aliases = {len(operands) + i: shift + i for i in range(3)}
        operands += list(state)
        specs += [vmem] * 3
    tiles = 2 * count + (3 if start else 0)
    return pl.pallas_call(
        functools.partial(group_kernel, inv, sizes, start, finish),
        out_shape=outs,
        in_specs=specs,
        out_specs=[vmem] * len(outs),
        scratch_shapes=[
            pltpu.VMEM((max(count, 1) * 512, 128), BF16),
            pltpu.VMEM((max(count, 1) * 512, 256), BF16),
            pltpu.VMEM((max(count, 1) * 2, 128), F32),
        ],
        input_output_aliases=aliases,
        compiler_params=pltpu.CompilerParams(vmem_limit_bytes=LIMIT),
        cost_estimate=pl.CostEstimate(
            flops=tiles * 2048 * 256 * 128 * 16,
            transcendentals=tiles * 2048 * 256,
            bytes_accessed=1 << 20,
        ),
        name=name,
    )(*operands)


def project_kernel(blocks, splits, first, columns, a_ref, w_ref, *o_refs):
    rows = jnp.concatenate([a_ref[b * 64 : (b + 1) * 64, :] for b in blocks], axis=0)
    for c in range(0, columns, TILE):
        product = jnp.dot(
            rows, w_ref[:, first + c : first + c + TILE], preferred_element_type=F32
        ).astype(BF16)
        at = 0
        for size, o_ref in zip(splits, o_refs):
            o_ref[:, c : c + TILE] = product[at * 64 : (at + size) * 64, :]
            at += size


def project(att, weight, blocks, splits, first, columns, name):
    vmem = pl.BlockSpec(memory_space=pltpu.VMEM)
    return pl.pallas_call(
        functools.partial(project_kernel, blocks, splits, first, columns),
        out_shape=[jax.ShapeDtypeStruct((s * 64, columns), BF16) for s in splits],
        in_specs=[vmem] * 2,
        out_specs=[vmem] * len(splits),
        compiler_params=pltpu.CompilerParams(vmem_limit_bytes=LIMIT),
        cost_estimate=pl.CostEstimate(
            flops=2 * len(blocks) * 64 * 1024 * columns,
            transcendentals=0,
            bytes_accessed=2 * 1024 * columns,
        ),
        name=name,
    )(att, weight)


def added(*arrays):
    total = arrays[0].astype(F32)
    for a in arrays[1:]:
        total = total + a.astype(F32)
    return total


def finish_kernel(cut, xo_ref, xf_ref, xb_ref, xl_ref, yo_ref, yy_ref, yf_ref, yb_ref, o_ref):
    o_ref[:, :cut] = added(xo_ref[0:64, :], xf_ref[0:64, :], xb_ref[0:64, :], xl_ref[...]).astype(
        BF16
    )
    o_ref[:, cut:] = added(yo_ref[192:256, :], yy_ref[192:256, :], yf_ref[...], yb_ref[...]).astype(
        BF16
    )


def scattered(att, weight, first_columns):
    rest = weight.shape[1] - first_columns
    (x_far,) = project(att, weight, (0, 1), (2,), 0, first_columns, "project_far")
    got_far = moved(x_far, ahead)
    (y_out,) = project(att, weight, (1, 3, 5, 7), (4,), first_columns, rest, "project_y")
    got_y = moved(y_out, beside)
    att, x_far, y_out = lax.optimization_barrier((att, x_far, y_out))
    x_ahead, x_own = project(att, weight, (2, 3, 6, 7), (2, 2), 0, first_columns, "project_c")
    att, x_ahead, x_own = lax.optimization_barrier((att, x_ahead, x_own))
    (x_behind,) = project(att, weight, (4, 5), (2,), 0, first_columns, "project_behind")
    got_front = moved(x_behind, behind)
    att, x_behind = lax.optimization_barrier((att, x_behind))
    (y_own,) = project(att, weight, (0, 2, 4, 6), (4,), first_columns, rest, "project_d")
    got_back = moved(added(x_ahead, got_far).astype(BF16), ahead)
    y_far, y_ahead, y_behind = [
        (y_own[i * 64 : (i + 1) * 64], got_y[i * 64 : (i + 1) * 64]) for i in range(3)
    ]
    x_out = added(x_own[64:], got_front[64:], got_back[64:]).astype(BF16)
    x_last = moved(x_out, beside)
    y_far_sum, y_behind_sum, x_out = lax.optimization_barrier(
        (added(*y_far).astype(BF16), added(*y_behind).astype(BF16), x_out)
    )
    y_got_far = moved(y_far_sum, ahead)
    y_got_front = moved(y_behind_sum, behind)
    y_got_back = moved(added(*y_ahead, y_got_far).astype(BF16), ahead)
    vmem = pl.BlockSpec(memory_space=pltpu.VMEM)
    return pl.pallas_call(
        functools.partial(finish_kernel, first_columns),
        out_shape=jax.ShapeDtypeStruct((64, first_columns + rest), BF16),
        in_specs=[vmem] * 8,
        out_specs=vmem,
        compiler_params=pltpu.CompilerParams(vmem_limit_bytes=LIMIT),
        name="finish",
    )(x_own, got_front, got_back, x_last, y_own, got_y, y_got_front, y_got_back)


def body(query, keys, values, k_scale, v_scale, block_place, out_weight):
    inv = math.log2(math.e) / math.sqrt(128)
    q = query.reshape(4096, 128)
    k = keys.reshape(512, 128)
    own = packed(k, values.reshape(512, 128), k_scale, v_scale, block_place)
    core = lax.axis_index("ctx") % 2
    place = lax.axis_index("head")
    target = jnp.arange(8, dtype=jnp.int32)
    along = (target % 4 - place % 4) % 4
    side = (target // 4 - place // 4) % 2
    forward = 1 + 2 * core
    slot = jnp.where(along == 0, 3, jnp.where(along == 2, 0, jnp.where(along == forward, 1, 2)))
    order = (slot * 2 + side).astype(jnp.int32)
    own, order = lax.optimization_barrier((own, order))
    partner = moved(own, swapped)
    pair = jnp.concatenate([own, partner], axis=0)
    one, two = moved(pair, near), moved(pair, across)
    state = attend(q, own, [], None, None, inv, "attend_own")
    pair, mine, *state = lax.optimization_barrier((pair, own, *state))
    three, four = moved(pair, diagonal), moved(mine, opposite)
    state = attend(q, own, [partner], state, None, inv, "attend_partner")
    one, two, *state = lax.optimization_barrier((one, two, *state))
    more = moved(jnp.concatenate([one, two], axis=0), swapped)
    state = attend(q, own, [one, two], state, None, inv, "attend_near")
    state = attend(q, own, [more], state, None, inv, "attend_more")
    three, four, *state = lax.optimization_barrier((three, four, *state))
    last = jnp.concatenate([three, four], axis=0)
    final = moved(last, swapped)
    state = attend(q, own, [last], state, None, inv, "attend_last")
    attended = attend(q, own, [final], state, order, inv, "attend_rest")[0]
    return scattered(attended, out_weight, 4864)


def solution(mesh):
    placed = (
        P("ctx", "head", None),
        P("ctx", "head", None),
        P("ctx", "head", None),
        P("ctx", "head"),
        P("ctx", "head"),
        P("ctx"),
        P("head", None),
    )
    return jax.shard_map(
        body, mesh=mesh, in_specs=placed, out_specs=P(("ctx", "head"), None), check_vma=False
    )
```
